256 devices in a mesh: gx: 32 (over z, x_lo, core), gy: 8 (over y, x_hi).
Axes of the slice: x: 4 (x_hi: 2, x_lo: 2; x = x_hi * 2 + x_lo), y: 4, z: 8, core: 2. Of those that a mesh axis runs over, the one named last changes fastest.
Arguments:
- fine_old: float32 [2, 3, 40, 64, 2048], P(None, None, None, 'gx', 'gy'), may hold values from -6 to 6
- fine_now: float32 [2, 3, 40, 64, 2048], P(None, None, None, 'gx', 'gy'), may hold values from -6 to 6
- coarse_old: float32 [2, 3, 80, 32, 1024], P(None, None, None, 'gx', 'gy'), may hold values from -6 to 6
- coarse_now: float32 [2, 3, 80, 32, 1024], P(None, None, None, 'gx', 'gy'), may hold values from -6 to 6
- shear_fine: float32 [40, 64, 2048], P(None, 'gx', 'gy'), may hold values from 0.3 to 1.2
- lame_fine: float32 [40, 64, 2048], P(None, 'gx', 'gy'), may hold values from 0.5 to 2
- shear_coarse: float32 [80, 32, 1024], P(None, 'gx', 'gy'), may hold values from 0.3 to 1.2
- lame_coarse: float32 [80, 32, 1024], P(None, 'gx', 'gy'), may hold values from 0.5 to 2
- topography: int32 [64, 2048], P('gx', 'gy'), may hold values from 0 to 512
Outputs:
- fine_field: float32 [2, 3, 40, 64, 2048], P(None, None, None, 'gx', 'gy')
- coarse_field: float32 [2, 3, 80, 32, 1024], P(None, None, None, 'gx', 'gy')
- fine_kernel: float32 [40, 64, 2048], P(None, 'gx', 'gy')
- coarse_kernel: float32 [80, 32, 1024], P(None, 'gx', 'gy')
The draws below stay inside these ranges and needn't reach their ends.
All inputs are finite; a program needn't handle non-finite values.
Results may differ from the reference program's by a relative error of at most 0.0003.
Values sent between devices are 32-bit elements; how exact they have to be, the bound alone decides.
No kernel may reach another device: no remote copies, remote signals or barrier semaphores. Data moves between devices by JAX's collectives and lax.ppermute only.
A program may use at most 64 MiB of HBM per device.

```python
import math
import jax
import jax.numpy as jnp
from jax import lax

FZ = 40
CZ = 80
FXD = 2
STEPS = 2
NX = 64
NY = 2048
NXC = 32
NYC = 1024


def plant(array, key, smallest, high):
    longest = array.shape.index(max(array.shape))
    spots = []
    for shift in (0, 1):
        where = [jax.random.randint(jax.random.fold_in(key, axis), (), 0, length) for axis, length in enumerate(array.shape)]
        where[longest] = (where[longest] + shift) % array.shape[longest]
        spots.append(tuple(where))
    return array.at[spots[0]].set(smallest).at[spots[1]].set(high)


def shard_levels(own_key, dims, split, least, largest):
    factor_of, own = 1.0, jax.random.fold_in(own_key, 6)
    for axis_at, parts in split:
        steps = jnp.exp(jax.random.uniform(jax.random.fold_in(own, axis_at), (parts,), jnp.float32, least / len(split), largest / len(split)))
        factor_of = factor_of * jnp.repeat(steps, dims[axis_at] // parts).reshape([-1 if axis == axis_at else 1 for axis in range(len(dims))])
    return factor_of


def gaussian(rng, extent, scale, reach, cuts=(), kind=jnp.bfloat16):
    array = scale * jax.random.normal(rng, extent, jnp.float32)
    if cuts:
        array = array * shard_levels(rng, extent, cuts, -0.22, 0.18)
    return jnp.clip(array, -reach, reach).astype(kind)


def setup_inputs(seed: int = 0) -> dict:
    keys = jax.random.split(jax.random.key(seed), 10)
    return {
        "fine_old": gaussian(keys[0], (2, 3, FZ, NX, NY), 1.0, 6.0, ((3, 32), (4, 8)), jnp.float32),
        "fine_now": gaussian(keys[1], (2, 3, FZ, NX, NY), 1.0, 6.0, ((3, 32), (4, 8)), jnp.float32),
        "coarse_old": gaussian(keys[2], (2, 3, CZ, NXC, NYC), 1.0, 6.0, ((3, 32), (4, 8)), jnp.float32),
        "coarse_now": gaussian(keys[3], (2, 3, CZ, NXC, NYC), 1.0, 6.0, ((3, 32), (4, 8)), jnp.float32),
        "shear_fine": jnp.clip(jnp.exp(math.log(1.2) - 1.3862944 * jax.random.uniform(keys[4], (FZ, NX, NY), jnp.float32) ** shard_levels(keys[4], (FZ, NX, NY), ((1, 32), (2, 8)), -0.2, 0.2)), 0.3, 1.2),
        "lame_fine": jnp.clip(jnp.exp(math.log(2.0) - 1.3862944 * jax.random.uniform(keys[5], (FZ, NX, NY), jnp.float32) ** shard_levels(keys[5], (FZ, NX, NY), ((1, 32), (2, 8)), -0.2, 0.2)), 0.5, 2.0),
        "shear_coarse": jnp.clip(jnp.exp(math.log(1.2) - 1.3862944 * jax.random.uniform(keys[6], (CZ, NXC, NYC), jnp.float32) ** shard_levels(keys[6], (CZ, NXC, NYC), ((1, 32), (2, 8)), -0.2, 0.2)), 0.3, 1.2),
        "lame_coarse": jnp.clip(jnp.exp(math.log(2.0) - 1.3862944 * jax.random.uniform(keys[7], (CZ, NXC, NYC), jnp.float32) ** shard_levels(keys[7], (CZ, NXC, NYC), ((1, 32), (2, 8)), -0.2, 0.2)), 0.5, 2.0),
        "topography": plant(jax.random.randint(keys[8], (NX, NY), 0, 513), jax.random.fold_in(keys[8], 1), 0, 512).astype(jnp.int32),
    }


STEP_SQUARED = 0.04


def offset(padded, up_down, along_x, along_y):
    depth_cells = padded.shape[2] - 2
    row_count = padded.shape[3] - 2
    column_count = padded.shape[4] - 2
    return padded[:, :, 1 + up_down:1 + up_down + depth_cells, 1 + along_x:1 + along_x + row_count, 1 + along_y:1 + along_y + column_count]


def accelerate(padded, spacing_pad, grid_step, shear, lame):
    center = offset(padded, 0, 0, 0)
    spacing = spacing_pad[1:-1, 1:-1]
    inverse_area = 1.0 / (grid_step * grid_step)
    curve_xx = (offset(padded, 0, 1, 0) - 2.0 * center + offset(padded, 0, -1, 0)) * inverse_area
    curve_yy = (offset(padded, 0, 0, 1) - 2.0 * center + offset(padded, 0, 0, -1)) * inverse_area
    curve_zz = (offset(padded, 1, 0, 0) - 2.0 * center + offset(padded, -1, 0, 0)) / (spacing * spacing)
    mixed_xy = (offset(padded, 0, 1, 1) - offset(padded, 0, 1, -1) - offset(padded, 0, -1, 1) + offset(padded, 0, -1, -1)) * (0.25 * inverse_area)
    east_side = (offset(padded, 1, 1, 0) - offset(padded, -1, 1, 0)) / (2.0 * spacing_pad[2:, 1:-1])
    west_side = (offset(padded, 1, -1, 0) - offset(padded, -1, -1, 0)) / (2.0 * spacing_pad[:-2, 1:-1])
    mixed_xz = (east_side - west_side) * (0.5 / grid_step)
    north_side = (offset(padded, 1, 0, 1) - offset(padded, -1, 0, 1)) / (2.0 * spacing_pad[1:-1, 2:])
    south_side = (offset(padded, 1, 0, -1) - offset(padded, -1, 0, -1)) / (2.0 * spacing_pad[1:-1, :-2])
    mixed_yz = (north_side - south_side) * (0.5 / grid_step)
    laplace = curve_xx + curve_yy + curve_zz
    grad_div = jnp.stack([
        curve_xx[:, 0] + mixed_xy[:, 1] + mixed_xz[:, 2],
        mixed_xy[:, 0] + curve_yy[:, 1] + mixed_yz[:, 2],
        mixed_xz[:, 0] + mixed_yz[:, 1] + curve_zz[:, 2]], axis=1)
    return shear * laplace + (lame + shear) * grad_div


def restrict(plane):
    row_sums = plane[..., 0::2, :] + plane[..., 1::2, :]
    summed = row_sums[..., 0::2] + row_sums[..., 1::2]
    return 0.25 * summed


def prolong(padded_plane):
    middle = 0.75 * padded_plane[..., 1:-1, :]
    even_rows = middle + 0.25 * padded_plane[..., :-2, :]
    odd_rows = middle + 0.25 * padded_plane[..., 2:, :]
    plane_dims = even_rows.shape
    row_pairs = jnp.stack([even_rows, odd_rows], axis=-2).reshape(plane_dims[:-2] + (2 * plane_dims[-2], plane_dims[-1]))
    center_cols = 0.75 * row_pairs[..., 1:-1]
    even_cols = center_cols + 0.25 * row_pairs[..., :-2]
    odd_cols = center_cols + 0.25 * row_pairs[..., 2:]
    col_dims = even_cols.shape
    return jnp.stack([even_cols, odd_cols], axis=-1).reshape(col_dims[:-1] + (2 * col_dims[-1],))


def pad_sides(block):
    return jnp.pad(block, ((0, 0), (0, 0), (0, 0), (1, 1), (1, 1)))


def blocked(padded, spacing_pad, grid_step, shear, lame, block_rows):
    block_count = (padded.shape[3] - 2) // block_rows

    def one_block(block_index):
        first_row = (block_index * block_rows).astype(jnp.int32)
        field_piece = lax.dynamic_slice_in_dim(padded, first_row, block_rows + 2, 3)
        space_piece = lax.dynamic_slice_in_dim(spacing_pad, first_row, block_rows + 2, 0)
        shear_piece = lax.dynamic_slice_in_dim(shear, first_row, block_rows, 1)
        lame_piece = lax.dynamic_slice_in_dim(lame, first_row, block_rows, 1)
        return accelerate(field_piece, space_piece, grid_step, shear_piece, lame_piece)

    pieces = lax.map(one_block, jnp.arange(block_count, dtype=jnp.int32))
    reordered = jnp.moveaxis(pieces, 0, 3)
    dims_now = reordered.shape
    return reordered.reshape(dims_now[:3] + (dims_now[3] * dims_now[4], dims_now[5]))


def reference(fine_old, fine_now, coarse_old, coarse_now, shear_fine, lame_fine, shear_coarse, lame_coarse, topography):
    heights = jnp.pad(topography.astype(jnp.float32), 1)
    fine_space = 1.0 + heights / 1024.0
    coarse_space = jnp.full((NXC + 2, NYC + 2), 2.0, jnp.float32)
    fine_kernel = jnp.zeros((FZ, NX, NY), jnp.float32)
    coarse_kernel = jnp.zeros((CZ, NXC, NYC), jnp.float32)
    for time_level in range(STEPS):
        ridge = restrict(fine_now[:, :, -1])
        floor_plane = jnp.zeros_like(ridge)
        coarse_ext = jnp.concatenate([ridge[:, :, None], coarse_now, floor_plane[:, :, None]], axis=2)
        coarse_pad = pad_sides(coarse_ext)
        ghost = prolong(coarse_pad[:, :, 1])
        fine_ext = jnp.concatenate([fine_now[:, :, :1], fine_now, ghost[:, :, None]], axis=2)
        fine_pad = pad_sides(fine_ext)
        fine_next = 2.0 * fine_now - fine_old + STEP_SQUARED * blocked(fine_pad, fine_space, 1.0, shear_fine, lame_fine, FXD)
        coarse_next = 2.0 * coarse_now - coarse_old + STEP_SQUARED * blocked(coarse_pad, coarse_space, 2.0, shear_coarse, lame_coarse, FXD // 2)
        fine_kernel = fine_kernel + jnp.sum(fine_next[0] * fine_next[1], axis=0)
        coarse_kernel = coarse_kernel + jnp.sum(coarse_next[0] * coarse_next[1], axis=0)
        fine_old, fine_now = fine_now, fine_next
        coarse_old, coarse_now = coarse_now, coarse_next
    return fine_now, coarse_now, fine_kernel, coarse_kernel
```

```python
import jax
import jax.numpy as jnp
import ml_dtypes
import numpy as np
from jax import lax
from jax.experimental import pallas as pl
from jax.experimental.pallas import tpu as pltpu
from jax.sharding import PartitionSpec as P

F = 6
FZ = 40
CZ = 80
L = 128
ZP = 8
DT2 = 0.04
F32 = jnp.float32

FINE_ROWS = F * FZ * 4
COARSE_ROWS = F * CZ
BULK = 2 * F * FZ + F * CZ + 8
RIDGE_AT = 2 * F * FZ + F * CZ
TOPO_AT = RIDGE_AT + F
VM = pl.BlockSpec(memory_space=pltpu.VMEM)
PARAMS = pltpu.CompilerParams(vmem_limit_bytes=48 * 1024 * 1024)


def pool_weights():
    w = np.zeros((384, 256), np.float32)
    for n in range(384):
        if n < 256:
            w[n, n // 2] = 0.25
        else:
            k = n - 256
            w[n, 128 + (k // 2 if k < 64 else 64 + k // 2)] = 0.25
    return w.astype(ml_dtypes.bfloat16)


def spread_weights():
    w = np.zeros((256, 384), np.float32)
    for n in range(384):
        col = n if n < 320 else n - 384
        j = col // 2
        w[j % 256, n] += 0.75
        w[(j + (1 if col % 2 else -1)) % 256, n] += 0.25
    return w.astype(ml_dtypes.bfloat16)


POOL = pool_weights()
SPREAD = spread_weights()


def exact_dot(rows, weights):
    hi = rows.astype(jnp.bfloat16)
    rest = rows - hi.astype(F32)
    mid = rest.astype(jnp.bfloat16)
    low = (rest - mid.astype(F32)).astype(jnp.bfloat16)
    dot = lambda part: jnp.dot(part, weights, preferred_element_type=F32)
    return dot(hi) + (dot(mid) + dot(low))


def lanes(shape):
    return lax.broadcasted_iota(jnp.int32, shape, len(shape) - 1)


def fine_rows(f, lt, x, start=0, size=FZ):
    return pl.ds((f * FZ + start) * 4 + lt * 2 + x, size, stride=4)


def coef_rows(lt, x, start=0, size=FZ):
    return pl.ds(start * 4 + lt * 2 + x, size, stride=4)


def first_pack(fn, fo, cn, co, sf, lf, sc, lc, tp, pool, mxa, mxb, mya, myb, tmp):
    px = lax.rem(lax.axis_index("gx"), 2)
    py = lax.rem(lax.axis_index("gy"), 2)
    tmp[...] = jnp.zeros_like(tmp)
    for f in range(F):
        for lt in range(2):
            tmp[f : f + 1, lt * L : (lt + 1) * L] = fn[pl.ds((f * FZ + FZ - 1) * 4 + lt * 2, 1), :] + fn[pl.ds((f * FZ + FZ - 1) * 4 + lt * 2 + 1, 1), :]
    ridge = exact_dot(tmp[...], pool[0:256, 0:L])
    for out, row in ((mxa, 1 - px), (mxb, px)):
        for f in range(F):
            for lt in range(2):
                out[f * 80 + lt * 40 : f * 80 + lt * 40 + 40, :] = fn[fine_rows(f, lt, row), :]
        out[480:960, :] = cn[...]
        out[RIDGE_AT : RIDGE_AT + 8, :] = ridge
        for lt in range(2):
            out[TOPO_AT + lt : TOPO_AT + lt + 1, :] = tp[pl.ds(lt * 2 + row, 1), :].astype(F32)
    group = lanes((FZ, L)) >> 2
    for out, right in ((mya, 1 - py), (myb, py)):
        base = 4 * right
        acc = jnp.zeros((FZ, L), F32)
        for arr, at in ((fn, 0), (fo, 12)):
            for f in range(F):
                for x in range(2):
                    g = at + f * 2 + x
                    acc = jnp.where(group == g, pltpu.roll(arr[fine_rows(f, right, x), :], lax.rem(base + 4 * g, L), 1), acc)
        for arr, at in ((sf, 24), (lf, 26)):
            for x in range(2):
                g = at + x
                acc = jnp.where(group == g, pltpu.roll(arr[coef_rows(right, x), :], lax.rem(base + 4 * g, L), 1), acc)
        for x in range(2):
            g = 28 + x
            plane = jnp.broadcast_to(tp[pl.ds(right * 2 + x, 1), :].astype(F32), (FZ, L))
            acc = jnp.where(group == g, pltpu.roll(plane, lax.rem(base + 4 * g, L), 1), acc)
        out[0:40, :] = acc
        acc = jnp.zeros((FZ, L), F32)
        for arr, at, count in ((cn, 0, F), (co, 12, F), (sc, 24, 1), (lc, 26, 1)):
            for f in range(count):
                for h in range(2):
                    g = at + f * 2 + h
                    acc = jnp.where(group == g, pltpu.roll(arr[f * CZ + h * 40 : f * CZ + h * 40 + 40, :], lax.rem(base + 4 * g, L), 1), acc)
        out[40:80, :] = acc


def open_y(rya, ryb, fn, pool, fh, foh, sh, th, ch, coh, sch, rg, mca, mcb, tmp):
    px = lax.rem(lax.axis_index("gx"), 2)
    py = lax.rem(lax.axis_index("gy"), 2)
    lane = lanes((FZ, L))
    in_a = ((lane + 4 * py) & 127) < 4
    in_b = ((lane + 4 * (1 - py)) & 127) < 4

    def halo(g, part):
        a = pltpu.roll(rya[part * 40 : part * 40 + 40, :], lax.rem(256 - 4 * g - 4 * py, L), 1)
        b = pltpu.roll(ryb[part * 40 : part * 40 + 40, :], lax.rem(256 - 4 * g - 4 * (1 - py), L), 1)
        return jnp.where(in_a, a, jnp.where(in_b, b, 0.0))

    for q in range(12):
        fh[q] = halo(q, 0)
        foh[q] = halo(12 + q, 0)
    for q in range(4):
        sh[q] = halo(24 + q, 0)
    for x in range(2):
        th[x] = halo(28 + x, 0)[0:8, :]
    for f in range(F):
        for h in range(2):
            ch[f, h * 40 : h * 40 + 40, :] = halo(f * 2 + h, 1)
            coh[f, h * 40 : h * 40 + 40, :] = halo(12 + f * 2 + h, 1)
    for q in range(2):
        for h in range(2):
            sch[q, h * 40 : h * 40 + 40, :] = halo(24 + q * 2 + h, 1)
    tmp[...] = jnp.zeros_like(tmp)
    for f in range(F):
        for lt in range(2):
            tmp[f : f + 1, lt * L : (lt + 1) * L] = fn[pl.ds((f * FZ + FZ - 1) * 4 + lt * 2, 1), :] + fn[pl.ds((f * FZ + FZ - 1) * 4 + lt * 2 + 1, 1), :]
        tmp[f : f + 1, 2 * L : 3 * L] = fh[f * 2, 39:40, :] + fh[f * 2 + 1, 39:40, :]
    rg[...] = exact_dot(tmp[...], pool[...])
    group = lane >> 3
    for out, row in ((mca, 1 - px), (mcb, px)):
        acc = jnp.zeros((FZ, L), F32)
        for f in range(F):
            acc = jnp.where(group == f, pltpu.roll(fh[f * 2 + row], 4 + 8 * f, 1), acc)
        acc = jnp.where(group == 6, pltpu.roll(jnp.broadcast_to(th[row, 0:1, :], (FZ, L)), 4 + 8 * 6, 1), acc)
        for f in range(F):
            g = 7 + f
            acc = jnp.where(group == g, pltpu.roll(jnp.broadcast_to(rg[f : f + 1, L : 2 * L], (FZ, L)), 4 + 8 * g, 1), acc)
        out[0:40, :] = acc
    acc = jnp.zeros((FZ, L), F32)
    for f in range(F):
        for h in range(2):
            g = f * 2 + h
            acc = jnp.where(group == g, pltpu.roll(ch[f, h * 40 : h * 40 + 40, :], (4 + 8 * g) % L, 1), acc)
    mca[40:80, :] = acc
    mcb[40:80, :] = acc


def ring_sum_diff(tiles_sum, tiles_diff, lane):
    def shifted(tiles):
        up = [pltpu.roll(t, L - 1, 1) for t in tiles]
        down = [pltpu.roll(t, 1, 1) for t in tiles]
        n = len(tiles)
        up = [jnp.where(lane < L - 1, up[t], up[(t + 1) % n]) for t in range(n)]
        down = [jnp.where(lane > 0, down[t], down[(t - 1) % n]) for t in range(n)]
        return up, down

    a, b = shifted(tiles_sum)
    c, d = shifted(tiles_diff)
    return [p + q for p, q in zip(a, b)], [p - q for p, q in zip(c, d)]


def vector_piece(load, own, nt, inv2j, invjj, h, lane):
    ia = 1.0 / (h * h)
    q = 0.25 * ia
    s = 0.5 / h
    cache = {}

    def u(i, r, t, dz=0):
        key = (i, r, t, dz)
        if key not in cache:
            cache[key] = load(i, r, t, dz)
        return cache[key]

    grads = {}

    def g(i, r, t):
        key = (i, r, t)
        if key not in grads:
            grads[key] = (u(i, r, t, 1) - u(i, r, t, -1)) * (inv2j(r, t) * s)
        return grads[key]

    out = {}
    ts = range(nt)
    for r in own:
        inner = (
            [q * (u(1, r + 1, t) - u(1, r - 1, t)) for t in ts],
            [q * (u(0, r + 1, t) - u(0, r - 1, t)) + g(2, r, t) for t in ts],
            [g(1, r, t) for t in ts],
        )
        for i in range(3):
            side, mixed = ring_sum_diff([u(i, r, t) for t in ts], inner[i], lane)
            for t in ts:
                c = u(i, r, t)
                c2 = c + c
                xx = (u(i, r + 1, t) + u(i, r - 1, t) - c2) * ia
                yy = (side[t] - c2) * ia
                zz = (u(i, r, t, 1) + u(i, r, t, -1) - c2) * invjj(r, t)
                cross = mixed[t]
                if i == 0:
                    cross = cross + (g(2, r + 1, t) - g(2, r - 1, t))
                if i == 2:
                    cross = cross + (g(0, r + 1, t) - g(0, r - 1, t))
                out[i, r, t] = (c2, xx + yy + zz, (xx, yy, zz)[i] + cross)
    return out


def interpolate(cc, spread, edges, lane8):
    left, right, low, high = edges
    a, b, c = cc[0], cc[1], cc[2]
    zero = jnp.zeros_like(a)
    mixes = [
        jnp.where(left, 0.75 * a + 0.25 * b, zero),
        0.75 * b + 0.25 * a,
        0.75 * b + 0.25 * c,
        jnp.where(right, 0.75 * c + 0.25 * b, zero),
    ]
    plane = exact_dot(jnp.concatenate(mixes, axis=0), spread[...])
    keep = (lane8 < 2 * L) | ((lane8 < 2 * L + 64) & high) | ((lane8 >= 2 * L + 64) & low)
    return jnp.where(keep, plane, 0.0)


def edges_here():
    x, y = lax.axis_index("gx"), lax.axis_index("gy")
    return x > 0, x < lax.axis_size("gx") - 1, y > 0, y < lax.axis_size("gy") - 1


def fill_ghosts(U, V, cc, spread, edges):
    for f in range(F):
        for r in range(3):
            for t in range(2):
                cc[r, f : f + 1, t * L : (t + 1) * L] = V[f, r, t, ZP : ZP + 1, :]
    plane = interpolate(cc, spread, edges, lanes((32, 384)))
    for f in range(F):
        for r in range(4):
            for t in range(3):
                U[f, r, t, ZP + FZ : ZP + FZ + 1, :] = plane[r * 8 + f : r * 8 + f + 1, t * L : (t + 1) * L]
                U[f, r, t, ZP - 1 : ZP, :] = U[f, r, t, ZP : ZP + 1, :]
        for r in range(3):
            for t in range(2):
                V[f, r, t, ZP + CZ : ZP + CZ + 1, :] = jnp.zeros((1, L), F32)


def step_one(
    fn, fo, cn, co, sf, lf, sc, lc, tp, fh, foh, sh, th, ch, coh, sch, rg, rxa, rxb, rca, rcb, spread, pool,
    f1, c1, rg1, mxa, mxb, jv, cf, cv, U, V, cc, tmp,
):
    px = lax.rem(lax.axis_index("gx"), 2)
    edges = edges_here()
    lane = lanes((8, L))
    lane40 = lanes((FZ, L))
    near40 = ((lane40 + 4) & 127) < 8

    def corner(rc, part, g):
        return jnp.where(near40, pltpu.roll(rc[part * 40 : part * 40 + 40, :], (2 * L - 4 - 8 * g) % L, 1), 0.0)

    cc[...] = jnp.zeros_like(cc)
    body = slice(ZP, ZP + FZ)
    for f in range(F):
        for x in range(2):
            for t in range(2):
                U[f, 1 + x, t, body, :] = fn[fine_rows(f, t, x), :]
            U[f, 1 + x, 2, body, :] = fh[f * 2 + x]
        V[f, 1, 0, ZP : ZP + CZ, :] = cn[f * CZ : (f + 1) * CZ, :]
        V[f, 1, 1, ZP : ZP + CZ, :] = ch[f]
        for t in range(2):
            V[f, 1, t, ZP - 1 : ZP, :] = rg[f : f + 1, t * L : (t + 1) * L]
    for rx, rc, fr, cr in ((rxa, rca, 3 * (1 - px), 2 * (1 - px)), (rxb, rcb, 3 * px, 2 * px)):
        for f in range(F):
            for t in range(2):
                U[f, fr, t, body, :] = rx[f * 80 + t * 40 : f * 80 + t * 40 + 40, :]
            U[f, fr, 2, body, :] = corner(rc, 0, f)
            V[f, cr, 0, ZP : ZP + CZ, :] = rx[480 + f * CZ : 480 + (f + 1) * CZ, :]
            for half in range(2):
                V[f, cr, 1, ZP + half * 40 : ZP + half * 40 + 40, :] = corner(rc, 1, f * 2 + half)
            V[f, cr, 0, ZP - 1 : ZP, :] = rx[RIDGE_AT + f : RIDGE_AT + f + 1, :]
            V[f, cr, 1, ZP - 1 : ZP, :] = corner(rc, 0, 7 + f)[0:1, :]
        for t in range(2):
            jv[0, fr, t] = jnp.broadcast_to(rx[TOPO_AT + t : TOPO_AT + t + 1, :], (8, L))
        jv[0, fr, 2] = corner(rc, 0, 6)[0:8, :]
    for x in range(2):
        for t in range(2):
            jv[0, 1 + x, t] = jnp.broadcast_to(tp[t * 2 + x : t * 2 + x + 1, :].astype(F32), (8, L))
        jv[0, 1 + x, 2] = th[x]
    for r in range(4):
        for t in range(3):
            spacing = 1.0 + jv[0, r, t] * (1.0 / 1024.0)
            jv[0, r, t] = 1.0 / (2.0 * spacing)
            jv[1, r, t] = 1.0 / (spacing * spacing)
    for x in range(2):
        for t in range(3):
            shear = sf[coef_rows(t, x), :] if t < 2 else sh[x]
            lame = lf[coef_rows(t, x), :] if t < 2 else sh[2 + x]
            cf[0, x, t] = DT2 * shear
            cf[1, x, t] = DT2 * (lame + shear)
    for t in range(2):
        shear = sc[...] if t == 0 else sch[0]
        lame = lc[...] if t == 0 else sch[1]
        cv[0, t] = DT2 * shear
        cv[1, t] = DT2 * (lame + shear)
    fill_ghosts(U, V, cc, spread, edges)
    keep = ((lane < 64) & edges[3]) | ((lane >= 64) & edges[2])

    def fine(a, _):
        for k in range(FZ // 8):
            at = ZP + 8 * k
            parts = vector_piece(
                lambda i, r, t, dz: U[a * 3 + i, r, t, at + dz : at + dz + 8, :], (1, 2), 3,
                lambda r, t: jv[0, r, t], lambda r, t: jv[1, r, t], 1.0, lane,
            )
            for (i, r, t), (c2, lap, gd) in parts.items():
                x = r - 1
                zs = slice(8 * k, 8 * k + 8)
                old = fo[fine_rows(a * 3 + i, t, x, 8 * k, 8), :] if t < 2 else foh[(a * 3 + i) * 2 + x, zs, :]
                new = c2 - old + cf[0, x, t, zs, :] * lap + cf[1, x, t, zs, :] * gd
                f1[(a * 3 + i) * 2 + x, t, zs, :] = new if t < 2 else jnp.where(keep, new, 0.0)
        return 0

    def coarse(a, _):
        for k in range(CZ // 8):
            at = ZP + 8 * k
            parts = vector_piece(
                lambda i, r, t, dz: V[a * 3 + i, r, t, at + dz : at + dz + 8, :], (1,), 2,
                lambda r, t: 0.25, lambda r, t: 0.25, 2.0, lane,
            )
            for (i, r, t), (c2, lap, gd) in parts.items():
                zs = slice(8 * k, 8 * k + 8)
                old = co[pl.ds((a * 3 + i) * CZ + 8 * k, 8), :] if t == 0 else coh[a * 3 + i, zs, :]
                new = c2 - old + cv[0, t, zs, :] * lap + cv[1, t, zs, :] * gd
                c1[a * 3 + i, t, zs, :] = new if t == 0 else jnp.where(keep, new, 0.0)
        return 0

    lax.fori_loop(0, 2, fine, 0)
    lax.fori_loop(0, 2, coarse, 0)
    tmp[...] = jnp.zeros_like(tmp)
    for f in range(F):
        for t in range(3):
            tmp[f : f + 1, t * L : (t + 1) * L] = f1[f * 2, t, FZ - 1 : FZ, :] + f1[f * 2 + 1, t, FZ - 1 : FZ, :]
    rg1[...] = exact_dot(tmp[...], pool[...])
    group = lane40 >> 2
    low = jnp.zeros((FZ, L), F32)
    for f in range(F):
        for half in range(2):
            g = 6 + 2 * f + half
            low = jnp.where(group == g, pltpu.roll(c1[f, 1, half * 40 : half * 40 + 40, :], 2 + 4 * g, 1), low)
    for out, row in ((mxa, 1 - px), (mxb, px)):
        acc = low
        for f in range(F):
            for t in range(2):
                out[f * 80 + t * 40 : f * 80 + t * 40 + 40, :] = f1[f * 2 + row, t]
            out[480 + f * CZ : 480 + (f + 1) * CZ, :] = c1[f, 0]
            acc = jnp.where(group == f, pltpu.roll(f1[f * 2 + row, 2], 2 + 4 * f, 1), acc)
        out[RIDGE_AT : RIDGE_AT + 8, :] = rg1[:, 0:L]
        out[BULK : BULK + 40, :] = acc


def step_two(fn, cn, f1, c1, rg1, rxa, rxb, jv, cf, cv, spread, fout, cout, fk, ck, U, V, cc):
    px = lax.rem(lax.axis_index("gx"), 2)
    edges = edges_here()
    lane = lanes((8, L))
    lane40 = lanes((FZ, L))
    near40 = ((lane40 + 2) & 127) < 4

    def corner(rx, g):
        return jnp.where(near40, pltpu.roll(rx[BULK : BULK + 40, :], (2 * L - 2 - 4 * g) % L, 1), 0.0)

    cc[...] = jnp.zeros_like(cc)
    body = slice(ZP, ZP + FZ)
    for f in range(F):
        for x in range(2):
            for t in range(3):
                U[f, 1 + x, t, body, :] = f1[f * 2 + x, t]
        for t in range(2):
            V[f, 1, t, ZP : ZP + CZ, :] = c1[f, t]
            V[f, 1, t, ZP - 1 : ZP, :] = rg1[f : f + 1, t * L : (t + 1) * L]
    for rx, fr, cr in ((rxa, 3 * (1 - px), 2 * (1 - px)), (rxb, 3 * px, 2 * px)):
        for f in range(F):
            for t in range(2):
                U[f, fr, t, body, :] = rx[f * 80 + t * 40 : f * 80 + t * 40 + 40, :]
            U[f, fr, 2, body, :] = corner(rx, f)
            V[f, cr, 0, ZP : ZP + CZ, :] = rx[480 + f * CZ : 480 + (f + 1) * CZ, :]
            for half in range(2):
                V[f, cr, 1, ZP + half * 40 : ZP + half * 40 + 40, :] = corner(rx, 6 + f * 2 + half)
            V[f, cr, 0, ZP - 1 : ZP, :] = rx[RIDGE_AT + f : RIDGE_AT + f + 1, :]
            V[f, cr, 1, ZP - 1 : ZP, :] = jnp.zeros((1, L), F32)
    fill_ghosts(U, V, cc, spread, edges)

    def fine(a, _):
        for k in range(FZ // 8):
            at = ZP + 8 * k
            parts = vector_piece(
                lambda i, r, t, dz: U[a * 3 + i, r, t, at + dz : at + dz + 8, :], (1, 2), 3,
                lambda r, t: jv[0, r, t], lambda r, t: jv[1, r, t], 1.0, lane,
            )
            for (i, r, t), (c2, lap, gd) in parts.items():
                if t < 2:
                    x = r - 1
                    zs = slice(8 * k, 8 * k + 8)
                    rows = fine_rows(a * 3 + i, t, x, 8 * k, 8)
                    fout[rows, :] = c2 - fn[rows, :] + cf[0, x, t, zs, :] * lap + cf[1, x, t, zs, :] * gd
        return 0

    def coarse(a, _):
        for k in range(CZ // 8):
            at = ZP + 8 * k
            parts = vector_piece(
                lambda i, r, t, dz: V[a * 3 + i, r, t, at + dz : at + dz + 8, :], (1,), 2,
                lambda r, t: 0.25, lambda r, t: 0.25, 2.0, lane,
            )
            for (i, r, t), (c2, lap, gd) in parts.items():
                if t == 0:
                    zs = slice(8 * k, 8 * k + 8)
                    rows = pl.ds((a * 3 + i) * CZ + 8 * k, 8)
                    cout[rows, :] = c2 - cn[rows, :] + cv[0, t, zs, :] * lap + cv[1, t, zs, :] * gd
        return 0

    lax.fori_loop(0, 2, fine, 0)
    lax.fori_loop(0, 2, coarse, 0)
    for x in range(2):
        for t in range(2):
            total = jnp.zeros((FZ, L), F32)
            for i in range(3):
                total = total + f1[i * 2 + x, t] * f1[(3 + i) * 2 + x, t]
            for i in range(3):
                total = total + fout[fine_rows(i, t, x), :] * fout[fine_rows(3 + i, t, x), :]
            fk[coef_rows(t, x), :] = total
    total = jnp.zeros((CZ, L), F32)
    for i in range(3):
        total = total + c1[i, 0] * c1[3 + i, 0]
    for i in range(3):
        total = total + cout[i * CZ : (i + 1) * CZ, :] * cout[(3 + i) * CZ : (4 + i) * CZ, :]
    ck[...] = total


def call(kernel, args, outs, scratch):
    shapes = tuple(jax.ShapeDtypeStruct(s, F32) for s in outs)
    return pl.pallas_call(
        kernel,
        out_shape=shapes,
        in_specs=[VM] * len(args),
        out_specs=(VM,) * len(outs),
        scratch_shapes=[pltpu.VMEM(s, F32) for s in scratch],
        compiler_params=PARAMS,
    )(*args)


def swap(cells, axis, first):
    count = lax.axis_size(axis)
    return lax.ppermute(cells, axis, [p for i in range(first, count - 1, 2) for p in ((i, i + 1), (i + 1, i))])


def rows_of(array):
    lead = array.size // 512
    return array.reshape(lead, 2, 2, L).transpose(0, 2, 1, 3).reshape(lead * 4, L)


def fine_of(rows, shape):
    return rows.reshape(-1, 2, 2, L).transpose(0, 2, 1, 3).reshape(shape)


def on_device(fine_old, fine_now, coarse_old, coarse_now, shear_fine, lame_fine, shear_coarse, lame_coarse, topography):
    fo, fn, sf, lf = rows_of(fine_old), rows_of(fine_now), rows_of(shear_fine), rows_of(lame_fine)
    tp = rows_of(topography)
    co, cn = coarse_old.reshape(-1, L), coarse_now.reshape(-1, L)
    sc, lc = shear_coarse.reshape(-1, L), lame_coarse.reshape(-1, L)
    pool, spread = jnp.asarray(POOL), jnp.asarray(SPREAD)
    mxa, mxb, mya, myb = call(first_pack, (fn, fo, cn, co, sf, lf, sc, lc, tp, pool), ((BULK, L), (BULK, L), (80, L), (80, L)), ((8, 256),))
    rxb = swap(mxb, "gx", 1)
    ryb = swap(myb, "gy", 1)
    rya = swap(mya, "gy", 0)
    rxa = swap(mxa, "gx", 0)
    fh, foh, sh, th, ch, coh, sch, rg, mca, mcb = call(
        open_y,
        (rya, ryb, fn, pool),
        ((12, FZ, L), (12, FZ, L), (4, FZ, L), (2, 8, L), (F, CZ, L), (F, CZ, L), (2, CZ, L), (8, 256), (80, L), (80, L)),
        ((8, 384),),
    )
    rcb = swap(mcb, "gx", 1)
    rca = swap(mca, "gx", 0)
    field = ((F, 4, 3, 56, L), (F, 3, 2, 96, L), (3, 8, 256))
    f1, c1, rg1, mxa, mxb, jv, cf, cv = call(
        step_one,
        (fn, fo, cn, co, sf, lf, sc, lc, tp, fh, foh, sh, th, ch, coh, sch, rg, rxa, rxb, rca, rcb, spread, pool),
        ((12, 3, FZ, L), (F, 2, CZ, L), (8, 256), (BULK + 40, L), (BULK + 40, L), (2, 4, 3, 8, L), (2, 2, 3, FZ, L), (2, 2, CZ, L)),
        field + ((8, 384),),
    )
    rxb = swap(mxb, "gx", 1)
    rxa = swap(mxa, "gx", 0)
    fout, cout, fk, ck = call(
        step_two,
        (fn, cn, f1, c1, rg1, rxa, rxb, jv, cf, cv, spread),
        ((FINE_ROWS, L), (COARSE_ROWS, L), (4 * FZ, L), (CZ, L)),
        field,
    )
    return (
        fine_of(fout, fine_now.shape),
        cout.reshape(coarse_now.shape),
        fine_of(fk, shear_fine.shape),
        ck.reshape(shear_coarse.shape),
    )


def solution(mesh):
    fields = P(None, None, None, "gx", "gy")
    cells = P(None, "gx", "gy")
    return jax.shard_map(
        on_device,
        mesh=mesh,
        in_specs=(fields, fields, fields, fields, cells, cells, cells, cells, P("gx", "gy")),
        out_specs=(fields, fields, cells, cells),
        check_vma=False,
    )
```

```python
import jax
import jax.numpy as jnp
import ml_dtypes
import numpy as np
from jax import lax
from jax.experimental import pallas as pl
from jax.experimental.pallas import tpu as pltpu
from jax.sharding import PartitionSpec as P

F = 6
FZ = 40
CZ = 80
L = 128
ZP = 8
DT2 = 0.04
F32 = jnp.float32

FINE_ROWS = F * FZ * 4
COARSE_ROWS = F * CZ
RIDGE_AT = 2 * F * FZ
TOPO_AT = RIDGE_AT + F
COARSE_AT = RIDGE_AT + 8
NEAR = COARSE_AT
BULK = COARSE_AT + COARSE_ROWS
VM = pl.BlockSpec(memory_space=pltpu.VMEM)


def pool_weights():
    w = np.zeros((384, 256), np.float32)
    for n in range(384):
        if n < 256:
            w[n, n // 2] = 0.25
        else:
            k = n - 256
            w[n, 128 + (k // 2 if k < 64 else 64 + k // 2)] = 0.25
    return w.astype(ml_dtypes.bfloat16)


def spread_weights():
    w = np.zeros((256, 384), np.float32)
    for n in range(384):
        col = n if n < 320 else n - 384
        j = col // 2
        w[j % 256, n] += 0.75
        w[(j + (1 if col % 2 else -1)) % 256, n] += 0.25
    return w.astype(ml_dtypes.bfloat16)


POOL = pool_weights()
SPREAD = spread_weights()


def exact_dot(rows, weights):
    hi = rows.astype(jnp.bfloat16)
    rest = rows - hi.astype(F32)
    mid = rest.astype(jnp.bfloat16)
    low = (rest - mid.astype(F32)).astype(jnp.bfloat16)
    dot = lambda part: jnp.dot(part, weights, preferred_element_type=F32)
    return dot(hi) + (dot(mid) + dot(low))


def lanes(shape):
    return lax.broadcasted_iota(jnp.int32, shape, len(shape) - 1)


def fine_rows(f, lt, x, start=0, size=FZ):
    return pl.ds((f * FZ + start) * 4 + lt * 2 + x, size, stride=4)


def coef_rows(lt, x, start=0, size=FZ):
    return pl.ds(start * 4 + lt * 2 + x, size, stride=4)


def load_and_pack_y(*refs):
    n = 11
    hbm, (fn, fo, cn, co, sf, lf, sc, lc, tp, pool, spread), (mxb, mya, myb, tmp, sems) = refs[:n], refs[n : 2 * n], refs[2 * n :]
    copies = [pltpu.make_async_copy(src, dst, sems.at[q]) for q, (src, dst) in enumerate(zip(hbm, refs[n : 2 * n]))]
    for copy in copies:
        copy.start()
    for copy in copies:
        copy.wait()
    pack_x(fn, cn, tp, pool, mxb, tmp)
    py = lax.rem(lax.axis_index("gy"), 2)
    group = lanes((FZ, L)) >> 2
    for out, right in ((mya, 1 - py), (myb, py)):
        base = 4 * right
        acc = jnp.zeros((FZ, L), F32)
        for arr, at in ((fn, 0), (fo, 12)):
            for f in range(F):
                for x in range(2):
                    g = at + f * 2 + x
                    acc = jnp.where(group == g, pltpu.roll(arr[fine_rows(f, right, x), :], lax.rem(base + 4 * g, L), 1), acc)
        for arr, at in ((sf, 24), (lf, 26)):
            for x in range(2):
                g = at + x
                acc = jnp.where(group == g, pltpu.roll(arr[coef_rows(right, x), :], lax.rem(base + 4 * g, L), 1), acc)
        for x in range(2):
            g = 28 + x
            plane = jnp.broadcast_to(tp[pl.ds(right * 2 + x, 1), :].astype(F32), (FZ, L))
            acc = jnp.where(group == g, pltpu.roll(plane, lax.rem(base + 4 * g, L), 1), acc)
        out[0:40, :] = acc
        acc = jnp.zeros((FZ, L), F32)
        for arr, at, count in ((cn, 0, F), (co, 12, F), (sc, 24, 1), (lc, 26, 1)):
            for f in range(count):
                for h in range(2):
                    g = at + f * 2 + h
                    acc = jnp.where(group == g, pltpu.roll(arr[f * CZ + h * 40 : f * CZ + h * 40 + 40, :], lax.rem(base + 4 * g, L), 1), acc)
        out[40:80, :] = acc


def bottom_sums(fn, tmp):
    for f in range(F):
        for lt in range(2):
            at = (f * FZ + FZ - 1) * 4 + lt * 2
            tmp[f : f + 1, lt * L : (lt + 1) * L] = fn[at : at + 1, :] + fn[at + 1 : at + 2, :]


def near_row(fn, tp, row, ridge, out):
    for f in range(F):
        for lt in range(2):
            out[f * 80 + lt * 40 : f * 80 + lt * 40 + 40, :] = fn[fine_rows(f, lt, row), :]
    out[RIDGE_AT : RIDGE_AT + 8, :] = ridge
    for lt in range(2):
        out[TOPO_AT + lt : TOPO_AT + lt + 1, :] = tp[pl.ds(lt * 2 + row, 1), :].astype(F32)


def pack_x(fn, cn, tp, pool, mxb, tmp):
    px = lax.rem(lax.axis_index("gx"), 2)
    tmp[...] = jnp.zeros_like(tmp)
    bottom_sums(fn, tmp)
    near_row(fn, tp, px, exact_dot(tmp[...], pool[0:256, 0:L]), mxb)
    mxb[COARSE_AT : COARSE_AT + COARSE_ROWS, :] = cn[...]


def open_y(rya, ryb, fn, tp, pool, fh, foh, sh, th, ch, coh, sch, rg, mxa, mcb, tmp):
    px = lax.rem(lax.axis_index("gx"), 2)
    py = lax.rem(lax.axis_index("gy"), 2)
    lane = lanes((FZ, L))
    in_a = ((lane + 4 * py) & 127) < 4
    in_b = ((lane + 4 * (1 - py)) & 127) < 4

    def halo(g, part):
        a = pltpu.roll(rya[part * 40 : part * 40 + 40, :], lax.rem(256 - 4 * g - 4 * py, L), 1)
        b = pltpu.roll(ryb[part * 40 : part * 40 + 40, :], lax.rem(256 - 4 * g - 4 * (1 - py), L), 1)
        return jnp.where(in_a, a, jnp.where(in_b, b, 0.0))

    for q in range(12):
        fh[q] = halo(q, 0)
        foh[q] = halo(12 + q, 0)
    for q in range(4):
        sh[q] = halo(24 + q, 0)
    for x in range(2):
        th[x] = halo(28 + x, 0)[0:8, :]
    for f in range(F):
        for h in range(2):
            ch[f, h * 40 : h * 40 + 40, :] = halo(f * 2 + h, 1)
            coh[f, h * 40 : h * 40 + 40, :] = halo(12 + f * 2 + h, 1)
    for q in range(2):
        for h in range(2):
            sch[q, h * 40 : h * 40 + 40, :] = halo(24 + q * 2 + h, 1)
    tmp[...] = jnp.zeros_like(tmp)
    bottom_sums(fn, tmp)
    for f in range(F):
        tmp[f : f + 1, 2 * L : 3 * L] = fh[f * 2, 39:40, :] + fh[f * 2 + 1, 39:40, :]
    rg[...] = exact_dot(tmp[...], pool[...])
    group = lane >> 3
    near_row(fn, tp, 1 - px, rg[:, 0:L], mxa)
    for out, at, row in ((mxa, NEAR, 1 - px), (mcb, 0, px)):
        acc = jnp.zeros((FZ, L), F32)
        for f in range(F):
            acc = jnp.where(group == f, pltpu.roll(fh[f * 2 + row], 4 + 8 * f, 1), acc)
        acc = jnp.where(group == 6, pltpu.roll(jnp.broadcast_to(th[row, 0:1, :], (FZ, L)), 4 + 8 * 6, 1), acc)
        for f in range(F):
            g = 7 + f
            acc = jnp.where(group == g, pltpu.roll(jnp.broadcast_to(rg[f : f + 1, L : 2 * L], (FZ, L)), 4 + 8 * g, 1), acc)
        out[at : at + 40, :] = acc
    acc = jnp.zeros((FZ, L), F32)
    for f in range(F):
        for h in range(2):
            g = f * 2 + h
            acc = jnp.where(group == g, pltpu.roll(ch[f, h * 40 : h * 40 + 40, :], (4 + 8 * g) % L, 1), acc)
    mxa[NEAR + 40 : NEAR + 80, :] = acc
    mcb[40:80, :] = acc


def ring_sum_diff(tiles_sum, tiles_diff, lane):
    def shifted(tiles):
        up = [pltpu.roll(t, L - 1, 1) for t in tiles]
        down = [pltpu.roll(t, 1, 1) for t in tiles]
        n = len(tiles)
        up = [jnp.where(lane < L - 1, up[t], up[(t + 1) % n]) for t in range(n)]
        down = [jnp.where(lane > 0, down[t], down[(t - 1) % n]) for t in range(n)]
        return up, down

    a, b = shifted(tiles_sum)
    c, d = shifted(tiles_diff)
    return [p + q for p, q in zip(a, b)], [p - q for p, q in zip(c, d)]


def vector_piece(load, own, nt, inv2j, invjj, h, lane):
    ia = 1.0 / (h * h)
    q = 0.25 * ia
    s = 0.5 / h
    cache = {}

    def u(i, r, t, dz=0):
        key = (i, r, t, dz)
        if key not in cache:
            cache[key] = load(i, r, t, dz)
        return cache[key]

    grads = {}

    def g(i, r, t):
        key = (i, r, t)
        if key not in grads:
            grads[key] = (u(i, r, t, 1) - u(i, r, t, -1)) * (inv2j(r, t) * s)
        return grads[key]

    out = {}
    ts = range(nt)
    for r in own:
        inner = (
            [q * (u(1, r + 1, t) - u(1, r - 1, t)) for t in ts],
            [q * (u(0, r + 1, t) - u(0, r - 1, t)) + g(2, r, t) for t in ts],
            [g(1, r, t) for t in ts],
        )
        for i in range(3):
            side, mixed = ring_sum_diff([u(i, r, t) for t in ts], inner[i], lane)
            for t in ts:
                c = u(i, r, t)
                c2 = c + c
                xx = (u(i, r + 1, t) + u(i, r - 1, t) - c2) * ia
                yy = (side[t] - c2) * ia
                zz = (u(i, r, t, 1) + u(i, r, t, -1) - c2) * invjj(r, t)
                cross = mixed[t]
                if i == 0:
                    cross = cross + (g(2, r + 1, t) - g(2, r - 1, t))
                if i == 2:
                    cross = cross + (g(0, r + 1, t) - g(0, r - 1, t))
                out[i, r, t] = (c2, xx + yy + zz, (xx, yy, zz)[i] + cross)
    return out


def interpolate(cc, spread, edges, lane8):
    left, right, low, high = edges
    a, b, c = cc[0], cc[1], cc[2]
    zero = jnp.zeros_like(a)
    mixes = [
        jnp.where(left, 0.75 * a + 0.25 * b, zero),
        0.75 * b + 0.25 * a,
        0.75 * b + 0.25 * c,
        jnp.where(right, 0.75 * c + 0.25 * b, zero),
    ]
    plane = exact_dot(jnp.concatenate(mixes, axis=0), spread[...])
    keep = (lane8 < 2 * L) | ((lane8 < 2 * L + 64) & high) | ((lane8 >= 2 * L + 64) & low)
    return jnp.where(keep, plane, 0.0)


def edges_here():
    x, y = lax.axis_index("gx"), lax.axis_index("gy")
    return x > 0, x < lax.axis_size("gx") - 1, y > 0, y < lax.axis_size("gy") - 1


def fill_ghosts(U, V, cc, spread, edges):
    for f in range(F):
        for r in range(3):
            for t in range(2):
                cc[r, f : f + 1, t * L : (t + 1) * L] = V[f, r, t, ZP : ZP + 1, :]
    plane = interpolate(cc, spread, edges, lanes((32, 384)))
    for f in range(F):
        for r in range(4):
            for t in range(3):
                U[f, r, t, ZP + FZ : ZP + FZ + 1, :] = plane[r * 8 + f : r * 8 + f + 1, t * L : (t + 1) * L]
                U[f, r, t, ZP - 1 : ZP, :] = U[f, r, t, ZP : ZP + 1, :]
        for r in range(3):
            for t in range(2):
                V[f, r, t, ZP + CZ : ZP + CZ + 1, :] = jnp.zeros((1, L), F32)


def step_one(
    fn, fo, cn, co, sf, lf, sc, lc, tp, fh, foh, sh, th, ch, coh, sch, rg, rxa, rac, rxb, rcb, spread, pool,
    f1, c1, rg1, mxa, mxb, jv, cf, cv, U, V, cc, tmp,
):
    px = lax.rem(lax.axis_index("gx"), 2)
    edges = edges_here()
    lane = lanes((8, L))
    lane40 = lanes((FZ, L))
    near40 = ((lane40 + 4) & 127) < 8

    def corner(rc, part, g):
        rc, at = rc
        return jnp.where(near40, pltpu.roll(rc[at + part * 40 : at + part * 40 + 40, :], (2 * L - 4 - 8 * g) % L, 1), 0.0)

    cc[...] = jnp.zeros_like(cc)
    body = slice(ZP, ZP + FZ)
    for f in range(F):
        for x in range(2):
            for t in range(2):
                U[f, 1 + x, t, body, :] = fn[fine_rows(f, t, x), :]
            U[f, 1 + x, 2, body, :] = fh[f * 2 + x]
        V[f, 1, 0, ZP : ZP + CZ, :] = cn[f * CZ : (f + 1) * CZ, :]
        V[f, 1, 1, ZP : ZP + CZ, :] = ch[f]
        for t in range(2):
            V[f, 1, t, ZP - 1 : ZP, :] = rg[f : f + 1, t * L : (t + 1) * L]
    for rx, rc, rz, zat, fr, cr in ((rxa, (rxa, NEAR), rac, 0, 3 * (1 - px), 2 * (1 - px)), (rxb, (rcb, 0), rxb, COARSE_AT, 3 * px, 2 * px)):
        for f in range(F):
            for t in range(2):
                U[f, fr, t, body, :] = rx[f * 80 + t * 40 : f * 80 + t * 40 + 40, :]
            U[f, fr, 2, body, :] = corner(rc, 0, f)
            V[f, cr, 0, ZP : ZP + CZ, :] = rz[zat + f * CZ : zat + (f + 1) * CZ, :]
            for half in range(2):
                V[f, cr, 1, ZP + half * 40 : ZP + half * 40 + 40, :] = corner(rc, 1, f * 2 + half)
            V[f, cr, 0, ZP - 1 : ZP, :] = rx[RIDGE_AT + f : RIDGE_AT + f + 1, :]
            V[f, cr, 1, ZP - 1 : ZP, :] = corner(rc, 0, 7 + f)[0:1, :]
        for t in range(2):
            jv[0, fr, t] = jnp.broadcast_to(rx[TOPO_AT + t : TOPO_AT + t + 1, :], (8, L))
        jv[0, fr, 2] = corner(rc, 0, 6)[0:8, :]
    for x in range(2):
        for t in range(2):
            jv[0, 1 + x, t] = jnp.broadcast_to(tp[t * 2 + x : t * 2 + x + 1, :].astype(F32), (8, L))
        jv[0, 1 + x, 2] = th[x]
    for r in range(4):
        for t in range(3):
            spacing = 1.0 + jv[0, r, t] * (1.0 / 1024.0)
            jv[0, r, t] = 1.0 / (2.0 * spacing)
            jv[1, r, t] = 1.0 / (spacing * spacing)
    for x in range(2):
        for t in range(3):
            shear = sf[coef_rows(t, x), :] if t < 2 else sh[x]
            lame = lf[coef_rows(t, x), :] if t < 2 else sh[2 + x]
            cf[0, x, t] = DT2 * shear
            cf[1, x, t] = DT2 * (lame + shear)
    for t in range(2):
        shear = sc[...] if t == 0 else sch[0]
        lame = lc[...] if t == 0 else sch[1]
        cv[0, t] = DT2 * shear
        cv[1, t] = DT2 * (lame + shear)
    fill_ghosts(U, V, cc, spread, edges)
    keep = ((lane < 64) & edges[3]) | ((lane >= 64) & edges[2])

    def fine(a, _):
        for k in range(FZ // 8):
            at = ZP + 8 * k
            parts = vector_piece(
                lambda i, r, t, dz: U[a * 3 + i, r, t, at + dz : at + dz + 8, :], (1, 2), 3,
                lambda r, t: jv[0, r, t], lambda r, t: jv[1, r, t], 1.0, lane,
            )
            for (i, r, t), (c2, lap, gd) in parts.items():
                x = r - 1
                zs = slice(8 * k, 8 * k + 8)
                old = fo[fine_rows(a * 3 + i, t, x, 8 * k, 8), :] if t < 2 else foh[(a * 3 + i) * 2 + x, zs, :]
                new = c2 - old + cf[0, x, t, zs, :] * lap + cf[1, x, t, zs, :] * gd
                f1[(a * 3 + i) * 2 + x, t, zs, :] = new if t < 2 else jnp.where(keep, new, 0.0)
        return 0

    def coarse(a, _):
        for k in range(CZ // 8):
            at = ZP + 8 * k
            parts = vector_piece(
                lambda i, r, t, dz: V[a * 3 + i, r, t, at + dz : at + dz + 8, :], (1,), 2,
                lambda r, t: 0.25, lambda r, t: 0.25, 2.0, lane,
            )
            for (i, r, t), (c2, lap, gd) in parts.items():
                zs = slice(8 * k, 8 * k + 8)
                old = co[pl.ds((a * 3 + i) * CZ + 8 * k, 8), :] if t == 0 else coh[a * 3 + i, zs, :]
                new = c2 - old + cv[0, t, zs, :] * lap + cv[1, t, zs, :] * gd
                c1[a * 3 + i, t, zs, :] = new if t == 0 else jnp.where(keep, new, 0.0)
        return 0

    lax.fori_loop(0, 2, fine, 0)
    lax.fori_loop(0, 2, coarse, 0)
    tmp[...] = jnp.zeros_like(tmp)
    for f in range(F):
        for t in range(3):
            tmp[f : f + 1, t * L : (t + 1) * L] = f1[f * 2, t, FZ - 1 : FZ, :] + f1[f * 2 + 1, t, FZ - 1 : FZ, :]
    rg1[...] = exact_dot(tmp[...], pool[...])
    group = lane40 >> 2
    low = jnp.zeros((FZ, L), F32)
    for f in range(F):
        for half in range(2):
            g = 6 + 2 * f + half
            low = jnp.where(group == g, pltpu.roll(c1[f, 1, half * 40 : half * 40 + 40, :], 2 + 4 * g, 1), low)
    for out, row in ((mxa, 1 - px), (mxb, px)):
        acc = low
        for f in range(F):
            for t in range(2):
                out[f * 80 + t * 40 : f * 80 + t * 40 + 40, :] = f1[f * 2 + row, t]
            out[COARSE_AT + f * CZ : COARSE_AT + (f + 1) * CZ, :] = c1[f, 0]
            acc = jnp.where(group == f, pltpu.roll(f1[f * 2 + row, 2], 2 + 4 * f, 1), acc)
        out[RIDGE_AT : RIDGE_AT + 8, :] = rg1[:, 0:L]
        out[BULK : BULK + 40, :] = acc


def step_two(fn, cn, f1, c1, rg1, rxa, rxb, jv, cf, cv, spread, fout, cout, fk, ck, U, V, cc):
    px = lax.rem(lax.axis_index("gx"), 2)
    edges = edges_here()
    lane = lanes((8, L))
    lane40 = lanes((FZ, L))
    near40 = ((lane40 + 2) & 127) < 4

    def corner(rx, g):
        return jnp.where(near40, pltpu.roll(rx[BULK : BULK + 40, :], (2 * L - 2 - 4 * g) % L, 1), 0.0)

    cc[...] = jnp.zeros_like(cc)
    body = slice(ZP, ZP + FZ)
    for f in range(F):
        for x in range(2):
            for t in range(3):
                U[f, 1 + x, t, body, :] = f1[f * 2 + x, t]
        for t in range(2):
            V[f, 1, t, ZP : ZP + CZ, :] = c1[f, t]
            V[f, 1, t, ZP - 1 : ZP, :] = rg1[f : f + 1, t * L : (t + 1) * L]
    for rx, fr, cr in ((rxa, 3 * (1 - px), 2 * (1 - px)), (rxb, 3 * px, 2 * px)):
        for f in range(F):
            for t in range(2):
                U[f, fr, t, body, :] = rx[f * 80 + t * 40 : f * 80 + t * 40 + 40, :]
            U[f, fr, 2, body, :] = corner(rx, f)
            V[f, cr, 0, ZP : ZP + CZ, :] = rx[COARSE_AT + f * CZ : COARSE_AT + (f + 1) * CZ, :]
            for half in range(2):
                V[f, cr, 1, ZP + half * 40 : ZP + half * 40 + 40, :] = corner(rx, 6 + f * 2 + half)
            V[f, cr, 0, ZP - 1 : ZP, :] = rx[RIDGE_AT + f : RIDGE_AT + f + 1, :]
            V[f, cr, 1, ZP - 1 : ZP, :] = jnp.zeros((1, L), F32)
    fill_ghosts(U, V, cc, spread, edges)

    def fine(a, _):
        for k in range(FZ // 8):
            at = ZP + 8 * k
            parts = vector_piece(
                lambda i, r, t, dz: U[a * 3 + i, r, t, at + dz : at + dz + 8, :], (1, 2), 3,
                lambda r, t: jv[0, r, t], lambda r, t: jv[1, r, t], 1.0, lane,
            )
            for (i, r, t), (c2, lap, gd) in parts.items():
                if t < 2:
                    x = r - 1
                    zs = slice(8 * k, 8 * k + 8)
                    rows = fine_rows(a * 3 + i, t, x, 8 * k, 8)
                    fout[rows, :] = c2 - fn[rows, :] + cf[0, x, t, zs, :] * lap + cf[1, x, t, zs, :] * gd
        return 0

    def coarse(a, _):
        for k in range(CZ // 8):
            at = ZP + 8 * k
            parts = vector_piece(
                lambda i, r, t, dz: V[a * 3 + i, r, t, at + dz : at + dz + 8, :], (1,), 2,
                lambda r, t: 0.25, lambda r, t: 0.25, 2.0, lane,
            )
            for (i, r, t), (c2, lap, gd) in parts.items():
                if t == 0:
                    zs = slice(8 * k, 8 * k + 8)
                    rows = pl.ds((a * 3 + i) * CZ + 8 * k, 8)
                    cout[rows, :] = c2 - cn[rows, :] + cv[0, t, zs, :] * lap + cv[1, t, zs, :] * gd
        return 0

    lax.fori_loop(0, 2, fine, 0)
    lax.fori_loop(0, 2, coarse, 0)
    for x in range(2):
        for t in range(2):
            total = jnp.zeros((FZ, L), F32)
            for i in range(3):
                total = total + f1[i * 2 + x, t] * f1[(3 + i) * 2 + x, t]
            for i in range(3):
                total = total + fout[fine_rows(i, t, x), :] * fout[fine_rows(3 + i, t, x), :]
            fk[coef_rows(t, x), :] = total
    total = jnp.zeros((CZ, L), F32)
    for i in range(3):
        total = total + c1[i, 0] * c1[3 + i, 0]
    for i in range(3):
        total = total + cout[i * CZ : (i + 1) * CZ, :] * cout[(3 + i) * CZ : (4 + i) * CZ, :]
    ck[...] = total


def call(kernel, args, outs, scratch, space=VM, megabytes=12):
    shapes = tuple(jax.ShapeDtypeStruct(s, F32) if isinstance(s, tuple) else s for s in outs)
    return pl.pallas_call(
        kernel,
        out_shape=shapes,
        in_specs=[space] * len(args),
        out_specs=(VM,) * len(outs),
        scratch_shapes=[pltpu.VMEM(s, F32) if isinstance(s, tuple) else s for s in scratch],
        compiler_params=pltpu.CompilerParams(vmem_limit_bytes=megabytes * 1024 * 1024),
    )(*args)


def swap(cells, axis, first):
    count = lax.axis_size(axis)
    return lax.ppermute(cells, axis, [p for i in range(first, count - 1, 2) for p in ((i, i + 1), (i + 1, i))])


def rows_of(array):
    lead = array.size // 512
    return array.reshape(lead, 2, 2, L).transpose(0, 2, 1, 3).reshape(lead * 4, L)


def fine_of(rows, shape):
    return rows.reshape(-1, 2, 2, L).transpose(0, 2, 1, 3).reshape(shape)


def on_device(fine_old, fine_now, coarse_old, coarse_now, shear_fine, lame_fine, shear_coarse, lame_coarse, topography):
    fo, fn, sf, lf = rows_of(fine_old), rows_of(fine_now), rows_of(shear_fine), rows_of(lame_fine)
    tp = rows_of(topography)
    co, cn = coarse_old.reshape(-1, L), coarse_now.reshape(-1, L)
    sc, lc = shear_coarse.reshape(-1, L), lame_coarse.reshape(-1, L)
    pool, spread = jnp.asarray(POOL), jnp.asarray(SPREAD)
    raw = (fn, fo, cn, co, sf, lf, sc, lc, tp, pool, spread)
    raw = tuple(pltpu.with_memory_space_constraint(v, pltpu.HBM) for v in raw)
    local = call(
        load_and_pack_y,
        raw,
        tuple(jax.ShapeDtypeStruct(v.shape, v.dtype) for v in raw) + ((BULK, L), (80, L), (80, L)),
        ((8, 256), pltpu.SemaphoreType.DMA((len(raw),)),),
        pl.BlockSpec(memory_space=pltpu.HBM),
    )
    fn, fo, cn, co, sf, lf, sc, lc, tp, pool, spread, mxb, mya, myb = local
    ryb = swap(myb, "gy", 1)
    rya = swap(mya, "gy", 0)
    rxb = swap(mxb, "gx", 1)
    fh, foh, sh, th, ch, coh, sch, rg, mxa, mcb = call(
        open_y,
        (rya, ryb, fn, tp, pool),
        ((12, FZ, L), (12, FZ, L), (4, FZ, L), (2, 8, L), (F, CZ, L), (F, CZ, L), (2, CZ, L), (8, 256), (NEAR + 80, L), (80, L)),
        ((8, 384),),
    )
    rcb = swap(mcb, "gx", 1)
    rxa = swap(mxa, "gx", 0)
    rac = swap(cn, "gx", 0)
    field = ((F, 4, 3, 56, L), (F, 3, 2, 96, L), (3, 8, 256))
    f1, c1, rg1, mxa, mxb, jv, cf, cv = call(
        step_one,
        (fn, fo, cn, co, sf, lf, sc, lc, tp, fh, foh, sh, th, ch, coh, sch, rg, rxa, rac, rxb, rcb, spread, pool),
        ((12, 3, FZ, L), (F, 2, CZ, L), (8, 256), (BULK + 40, L), (BULK + 40, L), (2, 4, 3, 8, L), (2, 2, 3, FZ, L), (2, 2, CZ, L)),
        field + ((8, 384),),
    )
    rxb = swap(mxb, "gx", 1)
    rxa = swap(mxa, "gx", 0)
    fout, cout, fk, ck = call(
        step_two,
        (fn, cn, f1, c1, rg1, rxa, rxb, jv, cf, cv, spread),
        ((FINE_ROWS, L), (COARSE_ROWS, L), (4 * FZ, L), (CZ, L)),
        field,
    )
    return (
        fine_of(fout, fine_now.shape),
        cout.reshape(coarse_now.shape),
        fine_of(fk, shear_fine.shape),
        ck.reshape(shear_coarse.shape),
    )


def solution(mesh):
    fields = P(None, None, None, "gx", "gy")
    cells = P(None, "gx", "gy")
    return jax.shard_map(
        on_device,
        mesh=mesh,
        in_specs=(fields, fields, fields, fields, cells, cells, cells, cells, P("gx", "gy")),
        out_specs=(fields, fields, cells, cells),
        check_vma=False,
    )
```

```python
import jax
import jax.numpy as jnp
import ml_dtypes
import numpy as np
from jax import lax
from jax.experimental import pallas as pl
from jax.experimental.pallas import tpu as pltpu
from jax.sharding import PartitionSpec as P

F = 6
FZ = 40
CZ = 80
L = 128
ZP = 8
DT2 = 0.04
F32 = jnp.float32

FINE_ROWS = F * FZ * 4
COARSE_ROWS = F * CZ
RIDGE_AT = 2 * F * FZ
TOPO_AT = RIDGE_AT + F
COARSE_AT = RIDGE_AT + 8
NEAR = COARSE_AT
BULK = COARSE_AT + COARSE_ROWS
LATER_COARSE = NEAR + 40
VM = pl.BlockSpec(memory_space=pltpu.VMEM)


def pool_weights():
    w = np.zeros((384, 256), np.float32)
    for n in range(384):
        if n < 256:
            w[n, n // 2] = 0.25
        else:
            k = n - 256
            w[n, 128 + (k // 2 if k < 64 else 64 + k // 2)] = 0.25
    return w.astype(ml_dtypes.bfloat16)


def spread_weights():
    w = np.zeros((256, 384), np.float32)
    for n in range(384):
        col = n if n < 320 else n - 384
        j = col // 2
        w[j % 256, n] += 0.75
        w[(j + (1 if col % 2 else -1)) % 256, n] += 0.25
    return w.astype(ml_dtypes.bfloat16)


POOL = pool_weights()
SPREAD = spread_weights()


def exact_dot(rows, weights):
    hi = rows.astype(jnp.bfloat16)
    rest = rows - hi.astype(F32)
    mid = rest.astype(jnp.bfloat16)
    low = (rest - mid.astype(F32)).astype(jnp.bfloat16)
    dot = lambda part: jnp.dot(part, weights, preferred_element_type=F32)
    return dot(hi) + (dot(mid) + dot(low))


def lanes(shape):
    return lax.broadcasted_iota(jnp.int32, shape, len(shape) - 1)


def fine_rows(f, lt, x, start=0, size=FZ):
    return pl.ds((f * FZ + start) * 4 + lt * 2 + x, size, stride=4)


def coef_rows(lt, x, start=0, size=FZ):
    return pl.ds(start * 4 + lt * 2 + x, size, stride=4)


def load_and_pack_y(*refs):
    n = 11
    hbm, (fn, fo, cn, co, sf, lf, sc, lc, tp, pool, spread), (mxb, mya, myb, tmp, sems) = refs[:n], refs[n : 2 * n], refs[2 * n :]
    copies = [pltpu.make_async_copy(src, dst, sems.at[q]) for q, (src, dst) in enumerate(zip(hbm, refs[n : 2 * n]))]
    for copy in copies:
        copy.start()
    for copy in copies:
        copy.wait()
    pack_x(fn, cn, tp, pool, mxb, tmp)
    py = lax.rem(lax.axis_index("gy"), 2)
    group = lanes((FZ, L)) >> 2
    for out, right in ((mya, 1 - py), (myb, py)):
        base = 4 * right
        acc = jnp.zeros((FZ, L), F32)
        for arr, at in ((fn, 0), (fo, 12)):
            for f in range(F):
                for x in range(2):
                    g = at + f * 2 + x
                    acc = jnp.where(group == g, pltpu.roll(arr[fine_rows(f, right, x), :], lax.rem(base + 4 * g, L), 1), acc)
        for arr, at in ((sf, 24), (lf, 26)):
            for x in range(2):
                g = at + x
                acc = jnp.where(group == g, pltpu.roll(arr[coef_rows(right, x), :], lax.rem(base + 4 * g, L), 1), acc)
        for x in range(2):
            g = 28 + x
            plane = jnp.broadcast_to(tp[pl.ds(right * 2 + x, 1), :].astype(F32), (FZ, L))
            acc = jnp.where(group == g, pltpu.roll(plane, lax.rem(base + 4 * g, L), 1), acc)
        out[0:40, :] = acc
        acc = jnp.zeros((FZ, L), F32)
        for arr, at, count in ((cn, 0, F), (co, 12, F), (sc, 24, 1), (lc, 26, 1)):
            for f in range(count):
                for h in range(2):
                    g = at + f * 2 + h
                    acc = jnp.where(group == g, pltpu.roll(arr[f * CZ + h * 40 : f * CZ + h * 40 + 40, :], lax.rem(base + 4 * g, L), 1), acc)
        out[40:80, :] = acc


def bottom_sums(fn, tmp):
    for f in range(F):
        for lt in range(2):
            at = (f * FZ + FZ - 1) * 4 + lt * 2
            tmp[f : f + 1, lt * L : (lt + 1) * L] = fn[at : at + 1, :] + fn[at + 1 : at + 2, :]


def near_row(fn, tp, row, ridge, out):
    for f in range(F):
        for lt in range(2):
            out[f * 80 + lt * 40 : f * 80 + lt * 40 + 40, :] = fn[fine_rows(f, lt, row), :]
    out[RIDGE_AT : RIDGE_AT + 8, :] = ridge
    for lt in range(2):
        out[TOPO_AT + lt : TOPO_AT + lt + 1, :] = tp[pl.ds(lt * 2 + row, 1), :].astype(F32)


def pack_x(fn, cn, tp, pool, mxb, tmp):
    px = lax.rem(lax.axis_index("gx"), 2)
    tmp[...] = jnp.zeros_like(tmp)
    bottom_sums(fn, tmp)
    near_row(fn, tp, px, exact_dot(tmp[...], pool[0:256, 0:L]), mxb)
    mxb[COARSE_AT : COARSE_AT + COARSE_ROWS, :] = cn[...]


def open_y(ryb, rya, fn, tp, pool, fh, foh, sh, th, ch, coh, sch, rg, mxa, mcb, tmp):
    px = lax.rem(lax.axis_index("gx"), 2)
    py = lax.rem(lax.axis_index("gy"), 2)
    lane = lanes((FZ, L))
    in_a = ((lane + 4 * py) & 127) < 4
    in_b = ((lane + 4 * (1 - py)) & 127) < 4

    def halo(g, part):
        a = pltpu.roll(rya[part * 40 : part * 40 + 40, :], lax.rem(256 - 4 * g - 4 * py, L), 1)
        b = pltpu.roll(ryb[part * 40 : part * 40 + 40, :], lax.rem(256 - 4 * g - 4 * (1 - py), L), 1)
        return jnp.where(in_a, a, jnp.where(in_b, b, 0.0))

    for q in range(12):
        fh[q] = halo(q, 0)
        foh[q] = halo(12 + q, 0)
    for q in range(4):
        sh[q] = halo(24 + q, 0)
    for x in range(2):
        th[x] = halo(28 + x, 0)[0:8, :]
    for f in range(F):
        for h in range(2):
            ch[f, h * 40 : h * 40 + 40, :] = halo(f * 2 + h, 1)
            coh[f, h * 40 : h * 40 + 40, :] = halo(12 + f * 2 + h, 1)
    for q in range(2):
        for h in range(2):
            sch[q, h * 40 : h * 40 + 40, :] = halo(24 + q * 2 + h, 1)
    tmp[...] = jnp.zeros_like(tmp)
    bottom_sums(fn, tmp)
    for f in range(F):
        tmp[f : f + 1, 2 * L : 3 * L] = fh[f * 2, 39:40, :] + fh[f * 2 + 1, 39:40, :]
    rg[...] = exact_dot(tmp[...], pool[...])
    group = lane >> 3
    near_row(fn, tp, 1 - px, rg[:, 0:L], mxa)
    for out, at, row in ((mxa, NEAR, 1 - px), (mcb, 0, px)):
        acc = jnp.zeros((FZ, L), F32)
        for f in range(F):
            acc = jnp.where(group == f, pltpu.roll(fh[f * 2 + row], 4 + 8 * f, 1), acc)
        acc = jnp.where(group == 6, pltpu.roll(jnp.broadcast_to(th[row, 0:1, :], (FZ, L)), 4 + 8 * 6, 1), acc)
        for f in range(F):
            g = 7 + f
            acc = jnp.where(group == g, pltpu.roll(jnp.broadcast_to(rg[f : f + 1, L : 2 * L], (FZ, L)), 4 + 8 * g, 1), acc)
        out[at : at + 40, :] = acc
    acc = jnp.zeros((FZ, L), F32)
    for f in range(F):
        for h in range(2):
            g = f * 2 + h
            acc = jnp.where(group == g, pltpu.roll(ch[f, h * 40 : h * 40 + 40, :], (4 + 8 * g) % L, 1), acc)
    mxa[NEAR + 40 : NEAR + 80, :] = acc
    mcb[40:80, :] = acc


def ring_sum_diff(tiles_sum, tiles_diff, lane):
    def shifted(tiles):
        up = [pltpu.roll(t, L - 1, 1) for t in tiles]
        down = [pltpu.roll(t, 1, 1) for t in tiles]
        n = len(tiles)
        up = [jnp.where(lane < L - 1, up[t], up[(t + 1) % n]) for t in range(n)]
        down = [jnp.where(lane > 0, down[t], down[(t - 1) % n]) for t in range(n)]
        return up, down

    a, b = shifted(tiles_sum)
    c, d = shifted(tiles_diff)
    return [p + q for p, q in zip(a, b)], [p - q for p, q in zip(c, d)]


def vector_piece(load, own, nt, inv2j, invjj, h, lane):
    ia = 1.0 / (h * h)
    q = 0.25 * ia
    s = 0.5 / h
    cache = {}

    def u(i, r, t, dz=0):
        key = (i, r, t, dz)
        if key not in cache:
            cache[key] = load(i, r, t, dz)
        return cache[key]

    grads = {}

    def g(i, r, t):
        key = (i, r, t)
        if key not in grads:
            grads[key] = (u(i, r, t, 1) - u(i, r, t, -1)) * (inv2j(r, t) * s)
        return grads[key]

    out = {}
    ts = range(nt)
    for r in own:
        inner = (
            [q * (u(1, r + 1, t) - u(1, r - 1, t)) for t in ts],
            [q * (u(0, r + 1, t) - u(0, r - 1, t)) + g(2, r, t) for t in ts],
            [g(1, r, t) for t in ts],
        )
        for i in range(3):
            side, mixed = ring_sum_diff([u(i, r, t) for t in ts], inner[i], lane)
            for t in ts:
                c = u(i, r, t)
                c2 = c + c
                xx = (u(i, r + 1, t) + u(i, r - 1, t) - c2) * ia
                yy = (side[t] - c2) * ia
                zz = (u(i, r, t, 1) + u(i, r, t, -1) - c2) * invjj(r, t)
                cross = mixed[t]
                if i == 0:
                    cross = cross + (g(2, r + 1, t) - g(2, r - 1, t))
                if i == 2:
                    cross = cross + (g(0, r + 1, t) - g(0, r - 1, t))
                out[i, r, t] = (c2, xx + yy + zz, (xx, yy, zz)[i] + cross)
    return out


def interpolate(cc, spread, edges, lane8):
    left, right, low, high = edges
    a, b, c = cc[0], cc[1], cc[2]
    zero = jnp.zeros_like(a)
    mixes = [
        jnp.where(left, 0.75 * a + 0.25 * b, zero),
        0.75 * b + 0.25 * a,
        0.75 * b + 0.25 * c,
        jnp.where(right, 0.75 * c + 0.25 * b, zero),
    ]
    plane = exact_dot(jnp.concatenate(mixes, axis=0), spread[...])
    keep = (lane8 < 2 * L) | ((lane8 < 2 * L + 64) & high) | ((lane8 >= 2 * L + 64) & low)
    return jnp.where(keep, plane, 0.0)


def edges_here():
    x, y = lax.axis_index("gx"), lax.axis_index("gy")
    return x > 0, x < lax.axis_size("gx") - 1, y > 0, y < lax.axis_size("gy") - 1


def fill_ghosts(U, V, cc, spread, edges):
    for f in range(F):
        for r in range(3):
            for t in range(2):
                cc[r, f : f + 1, t * L : (t + 1) * L] = V[f, r, t, ZP : ZP + 1, :]
    plane = interpolate(cc, spread, edges, lanes((32, 384)))
    for f in range(F):
        for r in range(4):
            for t in range(3):
                U[f, r, t, ZP + FZ : ZP + FZ + 1, :] = plane[r * 8 + f : r * 8 + f + 1, t * L : (t + 1) * L]
                U[f, r, t, ZP - 1 : ZP, :] = U[f, r, t, ZP : ZP + 1, :]
        for r in range(3):
            for t in range(2):
                V[f, r, t, ZP + CZ : ZP + CZ + 1, :] = jnp.zeros((1, L), F32)


def step_one(
    fn, fo, cn, co, sf, lf, sc, lc, tp, fh, foh, sh, th, ch, coh, sch, rg, rxa, rac, rxb, rcb, spread, pool,
    f1, c1, c1h, rg1, mxa, mxb, jv, cf, cv, U, V, cc, tmp,
):
    px = lax.rem(lax.axis_index("gx"), 2)
    edges = edges_here()
    lane = lanes((8, L))
    lane40 = lanes((FZ, L))
    near40 = ((lane40 + 4) & 127) < 8

    def corner(rc, part, g):
        rc, at = rc
        return jnp.where(near40, pltpu.roll(rc[at + part * 40 : at + part * 40 + 40, :], (2 * L - 4 - 8 * g) % L, 1), 0.0)

    cc[...] = jnp.zeros_like(cc)
    body = slice(ZP, ZP + FZ)
    for f in range(F):
        for x in range(2):
            for t in range(2):
                U[f, 1 + x, t, body, :] = fn[fine_rows(f, t, x), :]
            U[f, 1 + x, 2, body, :] = fh[f * 2 + x]
        V[f, 1, 0, ZP : ZP + CZ, :] = cn[f * CZ : (f + 1) * CZ, :]
        V[f, 1, 1, ZP : ZP + CZ, :] = ch[f]
        for t in range(2):
            V[f, 1, t, ZP - 1 : ZP, :] = rg[f : f + 1, t * L : (t + 1) * L]
    for rx, rc, rz, zat, fr, cr in ((rxa, (rxa, NEAR), rac, 0, 3 * (1 - px), 2 * (1 - px)), (rxb, (rcb, 0), rxb, COARSE_AT, 3 * px, 2 * px)):
        for f in range(F):
            for t in range(2):
                U[f, fr, t, body, :] = rx[f * 80 + t * 40 : f * 80 + t * 40 + 40, :]
            U[f, fr, 2, body, :] = corner(rc, 0, f)
            V[f, cr, 0, ZP : ZP + CZ, :] = rz[zat + f * CZ : zat + (f + 1) * CZ, :]
            for half in range(2):
                V[f, cr, 1, ZP + half * 40 : ZP + half * 40 + 40, :] = corner(rc, 1, f * 2 + half)
            V[f, cr, 0, ZP - 1 : ZP, :] = rx[RIDGE_AT + f : RIDGE_AT + f + 1, :]
            V[f, cr, 1, ZP - 1 : ZP, :] = corner(rc, 0, 7 + f)[0:1, :]
        for t in range(2):
            jv[0, fr, t] = jnp.broadcast_to(rx[TOPO_AT + t : TOPO_AT + t + 1, :], (8, L))
        jv[0, fr, 2] = corner(rc, 0, 6)[0:8, :]
    for x in range(2):
        for t in range(2):
            jv[0, 1 + x, t] = jnp.broadcast_to(tp[t * 2 + x : t * 2 + x + 1, :].astype(F32), (8, L))
        jv[0, 1 + x, 2] = th[x]
    for r in range(4):
        for t in range(3):
            spacing = 1.0 + jv[0, r, t] * (1.0 / 1024.0)
            jv[0, r, t] = 1.0 / (2.0 * spacing)
            jv[1, r, t] = 1.0 / (spacing * spacing)
    for x in range(2):
        for t in range(3):
            shear = sf[coef_rows(t, x), :] if t < 2 else sh[x]
            lame = lf[coef_rows(t, x), :] if t < 2 else sh[2 + x]
            cf[0, x, t] = DT2 * shear
            cf[1, x, t] = DT2 * (lame + shear)
    for t in range(2):
        shear = sc[...] if t == 0 else sch[0]
        lame = lc[...] if t == 0 else sch[1]
        cv[0, t] = DT2 * shear
        cv[1, t] = DT2 * (lame + shear)
    fill_ghosts(U, V, cc, spread, edges)
    keep = ((lane < 64) & edges[3]) | ((lane >= 64) & edges[2])

    def fine(a, _):
        for k in range(FZ // 8):
            at = ZP + 8 * k
            parts = vector_piece(
                lambda i, r, t, dz: U[a * 3 + i, r, t, at + dz : at + dz + 8, :], (1, 2), 3,
                lambda r, t: jv[0, r, t], lambda r, t: jv[1, r, t], 1.0, lane,
            )
            for (i, r, t), (c2, lap, gd) in parts.items():
                x = r - 1
                zs = slice(8 * k, 8 * k + 8)
                old = fo[fine_rows(a * 3 + i, t, x, 8 * k, 8), :] if t < 2 else foh[(a * 3 + i) * 2 + x, zs, :]
                new = c2 - old + cf[0, x, t, zs, :] * lap + cf[1, x, t, zs, :] * gd
                f1[(a * 3 + i) * 2 + x, t, zs, :] = new if t < 2 else jnp.where(keep, new, 0.0)
        return 0

    def coarse(a, _):
        for k in range(CZ // 8):
            at = ZP + 8 * k
            parts = vector_piece(
                lambda i, r, t, dz: V[a * 3 + i, r, t, at + dz : at + dz + 8, :], (1,), 2,
                lambda r, t: 0.25, lambda r, t: 0.25, 2.0, lane,
            )
            for (i, r, t), (c2, lap, gd) in parts.items():
                zs = slice(8 * k, 8 * k + 8)
                old = co[pl.ds((a * 3 + i) * CZ + 8 * k, 8), :] if t == 0 else coh[a * 3 + i, zs, :]
                new = c2 - old + cv[0, t, zs, :] * lap + cv[1, t, zs, :] * gd
                if t == 0:
                    c1[pl.ds((a * 3 + i) * CZ + 8 * k, 8), :] = new
                else:
                    c1h[a * 3 + i, zs, :] = jnp.where(keep, new, 0.0)
        return 0

    lax.fori_loop(0, 2, fine, 0)
    lax.fori_loop(0, 2, coarse, 0)
    tmp[...] = jnp.zeros_like(tmp)
    for f in range(F):
        for t in range(3):
            tmp[f : f + 1, t * L : (t + 1) * L] = f1[f * 2, t, FZ - 1 : FZ, :] + f1[f * 2 + 1, t, FZ - 1 : FZ, :]
    rg1[...] = exact_dot(tmp[...], pool[...])
    group = lane40 >> 2
    low = jnp.zeros((FZ, L), F32)
    for f in range(F):
        for half in range(2):
            g = 6 + 2 * f + half
            low = jnp.where(group == g, pltpu.roll(c1h[f, half * 40 : half * 40 + 40, :], 2 + 4 * g, 1), low)
    for out, row in ((mxa, 1 - px), (mxb, px)):
        acc = low
        for f in range(F):
            for t in range(2):
                out[f * 80 + t * 40 : f * 80 + t * 40 + 40, :] = f1[f * 2 + row, t]
            acc = jnp.where(group == f, pltpu.roll(f1[f * 2 + row, 2], 2 + 4 * f, 1), acc)
        out[RIDGE_AT : RIDGE_AT + 8, :] = rg1[:, 0:L]
        out[NEAR : NEAR + 40, :] = acc
    mxb[LATER_COARSE : LATER_COARSE + COARSE_ROWS, :] = c1[...]


def step_two(fn, cn, f1, c1, c1h, rg1, rxa, rac, rxb, jv, cf, cv, spread, fout, cout, fk, ck, U, V, cc):
    px = lax.rem(lax.axis_index("gx"), 2)
    edges = edges_here()
    lane = lanes((8, L))
    lane40 = lanes((FZ, L))
    near40 = ((lane40 + 2) & 127) < 4

    def corner(rx, g):
        return jnp.where(near40, pltpu.roll(rx[NEAR : NEAR + 40, :], (2 * L - 2 - 4 * g) % L, 1), 0.0)

    cc[...] = jnp.zeros_like(cc)
    body = slice(ZP, ZP + FZ)
    for f in range(F):
        for x in range(2):
            for t in range(3):
                U[f, 1 + x, t, body, :] = f1[f * 2 + x, t]
        V[f, 1, 0, ZP : ZP + CZ, :] = c1[f * CZ : (f + 1) * CZ, :]
        V[f, 1, 1, ZP : ZP + CZ, :] = c1h[f]
        for t in range(2):
            V[f, 1, t, ZP - 1 : ZP, :] = rg1[f : f + 1, t * L : (t + 1) * L]
    for rx, rz, zat, fr, cr in ((rxa, rac, 0, 3 * (1 - px), 2 * (1 - px)), (rxb, rxb, LATER_COARSE, 3 * px, 2 * px)):
        for f in range(F):
            for t in range(2):
                U[f, fr, t, body, :] = rx[f * 80 + t * 40 : f * 80 + t * 40 + 40, :]
            U[f, fr, 2, body, :] = corner(rx, f)
            V[f, cr, 0, ZP : ZP + CZ, :] = rz[zat + f * CZ : zat + (f + 1) * CZ, :]
            for half in range(2):
                V[f, cr, 1, ZP + half * 40 : ZP + half * 40 + 40, :] = corner(rx, 6 + f * 2 + half)
            V[f, cr, 0, ZP - 1 : ZP, :] = rx[RIDGE_AT + f : RIDGE_AT + f + 1, :]
            V[f, cr, 1, ZP - 1 : ZP, :] = jnp.zeros((1, L), F32)
    fill_ghosts(U, V, cc, spread, edges)

    def fine(a, _):
        for k in range(FZ // 8):
            at = ZP + 8 * k
            parts = vector_piece(
                lambda i, r, t, dz: U[a * 3 + i, r, t, at + dz : at + dz + 8, :], (1, 2), 3,
                lambda r, t: jv[0, r, t], lambda r, t: jv[1, r, t], 1.0, lane,
            )
            for (i, r, t), (c2, lap, gd) in parts.items():
                if t < 2:
                    x = r - 1
                    zs = slice(8 * k, 8 * k + 8)
                    rows = fine_rows(a * 3 + i, t, x, 8 * k, 8)
                    fout[rows, :] = c2 - fn[rows, :] + cf[0, x, t, zs, :] * lap + cf[1, x, t, zs, :] * gd
        return 0

    def coarse(a, _):
        for k in range(CZ // 8):
            at = ZP + 8 * k
            parts = vector_piece(
                lambda i, r, t, dz: V[a * 3 + i, r, t, at + dz : at + dz + 8, :], (1,), 2,
                lambda r, t: 0.25, lambda r, t: 0.25, 2.0, lane,
            )
            for (i, r, t), (c2, lap, gd) in parts.items():
                if t == 0:
                    zs = slice(8 * k, 8 * k + 8)
                    rows = pl.ds((a * 3 + i) * CZ + 8 * k, 8)
                    cout[rows, :] = c2 - cn[rows, :] + cv[0, t, zs, :] * lap + cv[1, t, zs, :] * gd
        return 0

    lax.fori_loop(0, 2, fine, 0)
    lax.fori_loop(0, 2, coarse, 0)
    for x in range(2):
        for t in range(2):
            total = jnp.zeros((FZ, L), F32)
            for i in range(3):
                total = total + f1[i * 2 + x, t] * f1[(3 + i) * 2 + x, t]
            for i in range(3):
                total = total + fout[fine_rows(i, t, x), :] * fout[fine_rows(3 + i, t, x), :]
            fk[coef_rows(t, x), :] = total
    total = jnp.zeros((CZ, L), F32)
    for i in range(3):
        total = total + c1[i * CZ : (i + 1) * CZ, :] * c1[(3 + i) * CZ : (4 + i) * CZ, :]
    for i in range(3):
        total = total + cout[i * CZ : (i + 1) * CZ, :] * cout[(3 + i) * CZ : (4 + i) * CZ, :]
    ck[...] = total


def call(kernel, args, outs, scratch, space=VM, megabytes=12, flops=0):
    shapes = tuple(jax.ShapeDtypeStruct(s, F32) if isinstance(s, tuple) else s for s in outs)
    return pl.pallas_call(
        kernel,
        out_shape=shapes,
        in_specs=[space] * len(args),
        out_specs=(VM,) * len(outs),
        scratch_shapes=[pltpu.VMEM(s, F32) if isinstance(s, tuple) else s for s in scratch],
        cost_estimate=pl.CostEstimate(flops=flops, transcendentals=0, bytes_accessed=1024) if flops else None,
        compiler_params=pltpu.CompilerParams(vmem_limit_bytes=megabytes * 1024 * 1024),
    )(*args)


def swap(cells, axis, first):
    count = lax.axis_size(axis)
    return lax.ppermute(cells, axis, [p for i in range(first, count - 1, 2) for p in ((i, i + 1), (i + 1, i))])


def rows_of(array):
    lead = array.size // 512
    return array.reshape(lead, 2, 2, L).transpose(0, 2, 1, 3).reshape(lead * 4, L)


def fine_of(rows, shape):
    return rows.reshape(-1, 2, 2, L).transpose(0, 2, 1, 3).reshape(shape)


def on_device(fine_old, fine_now, coarse_old, coarse_now, shear_fine, lame_fine, shear_coarse, lame_coarse, topography):
    fo, fn, sf, lf = rows_of(fine_old), rows_of(fine_now), rows_of(shear_fine), rows_of(lame_fine)
    tp = rows_of(topography)
    co, cn = coarse_old.reshape(-1, L), coarse_now.reshape(-1, L)
    sc, lc = shear_coarse.reshape(-1, L), lame_coarse.reshape(-1, L)
    pool, spread = jnp.asarray(POOL), jnp.asarray(SPREAD)
    raw = (fn, fo, cn, co, sf, lf, sc, lc, tp, pool, spread)
    raw = tuple(pltpu.with_memory_space_constraint(v, pltpu.HBM) for v in raw)
    local = call(
        load_and_pack_y,
        raw,
        tuple(jax.ShapeDtypeStruct(v.shape, v.dtype) for v in raw) + ((BULK, L), (80, L), (80, L)),
        ((8, 256), pltpu.SemaphoreType.DMA((len(raw),)),),
        pl.BlockSpec(memory_space=pltpu.HBM),
    )
    fn, fo, cn, co, sf, lf, sc, lc, tp, pool, spread, mxb, mya, myb = local
    ryb = swap(myb, "gy", 1)
    rya = swap(mya, "gy", 0)
    rxb = swap(mxb, "gx", 1)
    fh, foh, sh, th, ch, coh, sch, rg, mxa, mcb = call(
        open_y,
        (ryb, rya, fn, tp, pool),
        ((12, FZ, L), (12, FZ, L), (4, FZ, L), (2, 8, L), (F, CZ, L), (F, CZ, L), (2, CZ, L), (8, 256), (NEAR + 80, L), (80, L)),
        ((8, 384),),
        flops=5 * 10**9,
    )
    rcb = swap(mcb, "gx", 1)
    rxa = swap(mxa, "gx", 0)
    rac = swap(cn, "gx", 0)
    field = ((F, 4, 3, 56, L), (F, 3, 2, 96, L), (3, 8, 256))
    f1, c1, c1h, rg1, mxa, mxb, jv, cf, cv = call(
        step_one,
        (fn, fo, cn, co, sf, lf, sc, lc, tp, fh, foh, sh, th, ch, coh, sch, rg, rxa, rac, rxb, rcb, spread, pool),
        ((12, 3, FZ, L), (COARSE_ROWS, L), (F, CZ, L), (8, 256), (NEAR + 40, L), (BULK + 40, L), (2, 4, 3, 8, L), (2, 2, 3, FZ, L), (2, 2, CZ, L)),
        field + ((8, 384),),
    )
    rxb = swap(mxb, "gx", 1)
    rxa = swap(mxa, "gx", 0)
    rac = swap(c1, "gx", 0)
    fout, cout, fk, ck = call(
        step_two,
        (fn, cn, f1, c1, c1h, rg1, rxa, rac, rxb, jv, cf, cv, spread),
        ((FINE_ROWS, L), (COARSE_ROWS, L), (4 * FZ, L), (CZ, L)),
        field,
    )
    return (
        fine_of(fout, fine_now.shape),
        cout.reshape(coarse_now.shape),
        fine_of(fk, shear_fine.shape),
        ck.reshape(shear_coarse.shape),
    )


def solution(mesh):
    fields = P(None, None, None, "gx", "gy")
    cells = P(None, "gx", "gy")
    return jax.shard_map(
        on_device,
        mesh=mesh,
        in_specs=(fields, fields, fields, fields, cells, cells, cells, cells, P("gx", "gy")),
        out_specs=(fields, fields, cells, cells),
        check_vma=False,
    )
```

```python
import jax
import jax.numpy as jnp
import ml_dtypes
import numpy as np
from jax import lax
from jax.experimental import pallas as pl
from jax.experimental.pallas import tpu as pltpu
from jax.sharding import PartitionSpec as P

F = 6
FZ = 40
CZ = 80
L = 128
ZP = 8
DT2 = 0.04
F32 = jnp.float32

FINE_ROWS = F * FZ * 4
COARSE_ROWS = F * CZ
HFINE = 3 * 2 * FZ
HTOPO = HFINE + 3
HCOARSE = HFINE + 8
HALF = HCOARSE + 3 * CZ
HLATER = HCOARSE + 40
C_OPEN = 5*10**9
C_ONE = (5*10**9, 10**9)
C_TWO = 1
VM = pl.BlockSpec(memory_space=pltpu.VMEM)


def pool_weights():
    w = np.zeros((384, 256), np.float32)
    for n in range(384):
        if n < 256:
            w[n, n // 2] = 0.25
        else:
            k = n - 256
            w[n, 128 + (k // 2 if k < 64 else 64 + k // 2)] = 0.25
    return w.astype(ml_dtypes.bfloat16)


def spread_weights():
    w = np.zeros((256, 384), np.float32)
    for n in range(384):
        col = n if n < 320 else n - 384
        j = col // 2
        w[j % 256, n] += 0.75
        w[(j + (1 if col % 2 else -1)) % 256, n] += 0.25
    return w.astype(ml_dtypes.bfloat16)


POOL = pool_weights()
SPREAD = spread_weights()


def exact_dot(rows, weights):
    hi = rows.astype(jnp.bfloat16)
    rest = rows - hi.astype(F32)
    mid = rest.astype(jnp.bfloat16)
    low = (rest - mid.astype(F32)).astype(jnp.bfloat16)
    dot = lambda part: jnp.dot(part, weights, preferred_element_type=F32)
    return dot(hi) + (dot(mid) + dot(low))


def lanes(shape):
    return lax.broadcasted_iota(jnp.int32, shape, len(shape) - 1)


def fine_rows(f, lt, x, start=0, size=FZ):
    return pl.ds((f * FZ + start) * 4 + lt * 2 + x, size, stride=4)


def coef_rows(lt, x, start=0, size=FZ):
    return pl.ds(start * 4 + lt * 2 + x, size, stride=4)


def load_and_pack_y(*refs):
    n = 11
    hbm, (fn, fo, cn, co, sf, lf, sc, lc, tp, pool, spread), (ma, mbf, mbg, mya, myb, tmp, sems) = refs[:n], refs[n : 2 * n], refs[2 * n :]
    copies = [pltpu.make_async_copy(src, dst, sems.at[q]) for q, (src, dst) in enumerate(zip(hbm, refs[n : 2 * n]))]
    for copy in copies:
        copy.start()
    for copy in copies:
        copy.wait()
    pack_x(fn, cn, tp, pool, (ma, mbf, mbg), tmp)
    py = lax.rem(lax.axis_index("gy"), 2)
    group = lanes((FZ, L)) >> 2
    for out, right in ((mya, 1 - py), (myb, py)):
        base = 4 * right
        acc = jnp.zeros((FZ, L), F32)
        for arr, at in ((fn, 0), (fo, 12)):
            for f in range(F):
                for x in range(2):
                    g = at + f * 2 + x
                    acc = jnp.where(group == g, pltpu.roll(arr[fine_rows(f, right, x), :], lax.rem(base + 4 * g, L), 1), acc)
        for arr, at in ((sf, 24), (lf, 26)):
            for x in range(2):
                g = at + x
                acc = jnp.where(group == g, pltpu.roll(arr[coef_rows(right, x), :], lax.rem(base + 4 * g, L), 1), acc)
        for x in range(2):
            g = 28 + x
            plane = jnp.broadcast_to(tp[pl.ds(right * 2 + x, 1), :].astype(F32), (FZ, L))
            acc = jnp.where(group == g, pltpu.roll(plane, lax.rem(base + 4 * g, L), 1), acc)
        out[0:40, :] = acc
        acc = jnp.zeros((FZ, L), F32)
        for arr, at, count in ((cn, 0, F), (co, 12, F), (sc, 24, 1), (lc, 26, 1)):
            for f in range(count):
                for h in range(2):
                    g = at + f * 2 + h
                    acc = jnp.where(group == g, pltpu.roll(arr[f * CZ + h * 40 : f * CZ + h * 40 + 40, :], lax.rem(base + 4 * g, L), 1), acc)
        out[40:80, :] = acc


def bottom_sums(fn, tmp):
    for f in range(F):
        for lt in range(2):
            at = (f * FZ + FZ - 1) * 4 + lt * 2
            tmp[f : f + 1, lt * L : (lt + 1) * L] = fn[at : at + 1, :] + fn[at + 1 : at + 2, :]


def pack_x(fn, cn, tp, pool, outs, tmp):
    px = lax.rem(lax.axis_index("gx"), 2)
    tmp[...] = jnp.zeros_like(tmp)
    bottom_sums(fn, tmp)
    ridge = exact_dot(tmp[...], pool[0:256, 0:L])
    ma, mbf, mbg = outs
    in_chip = (ma.at[0:HALF, :], ma.at[HALF : 2 * HALF, :])
    for out, a, row in zip((*in_chip, mbf, mbg), (0, 1, 0, 1), (1 - px, 1 - px, px, px)):
        for i in range(3):
            for lt in range(2):
                out[i * 80 + lt * 40 : i * 80 + lt * 40 + 40, :] = fn[fine_rows(a * 3 + i, lt, row), :]
        out[HFINE : HFINE + 3, :] = ridge[a * 3 : a * 3 + 3, :]
        for lt in range(2):
            out[HTOPO + lt : HTOPO + lt + 1, :] = tp[pl.ds(lt * 2 + row, 1), :].astype(F32)
        out[HTOPO + 2 : HCOARSE, :] = jnp.zeros((3, L), F32)
        out[HCOARSE : HCOARSE + 3 * CZ, :] = cn[a * 3 * CZ : (a + 1) * 3 * CZ, :]
        if out.shape[0] > HALF:
            out[HALF : HALF + 8, :] = jnp.zeros((8, L), F32)


def open_y(ryb, rya, fn, pool, fh, foh, sh, th, ch, coh, sch, rg, mca, mcb, tmp):
    px = lax.rem(lax.axis_index("gx"), 2)
    py = lax.rem(lax.axis_index("gy"), 2)
    lane = lanes((FZ, L))
    in_a = ((lane + 4 * py) & 127) < 4
    in_b = ((lane + 4 * (1 - py)) & 127) < 4

    def halo(g, part):
        a = pltpu.roll(rya[part * 40 : part * 40 + 40, :], lax.rem(256 - 4 * g - 4 * py, L), 1)
        b = pltpu.roll(ryb[part * 40 : part * 40 + 40, :], lax.rem(256 - 4 * g - 4 * (1 - py), L), 1)
        return jnp.where(in_a, a, jnp.where(in_b, b, 0.0))

    for q in range(12):
        fh[q] = halo(q, 0)
        foh[q] = halo(12 + q, 0)
    for q in range(4):
        sh[q] = halo(24 + q, 0)
    for x in range(2):
        th[x] = halo(28 + x, 0)[0:8, :]
    for f in range(F):
        for h in range(2):
            ch[f, h * 40 : h * 40 + 40, :] = halo(f * 2 + h, 1)
            coh[f, h * 40 : h * 40 + 40, :] = halo(12 + f * 2 + h, 1)
    for q in range(2):
        for h in range(2):
            sch[q, h * 40 : h * 40 + 40, :] = halo(24 + q * 2 + h, 1)
    tmp[...] = jnp.zeros_like(tmp)
    bottom_sums(fn, tmp)
    for f in range(F):
        tmp[f : f + 1, 2 * L : 3 * L] = fh[f * 2, 39:40, :] + fh[f * 2 + 1, 39:40, :]
    rg[...] = exact_dot(tmp[...], pool[...])
    group = lane >> 3
    for out, row in ((mca, 1 - px), (mcb, px)):
        acc = jnp.zeros((FZ, L), F32)
        for f in range(F):
            acc = jnp.where(group == f, pltpu.roll(fh[f * 2 + row], 4 + 8 * f, 1), acc)
        acc = jnp.where(group == 6, pltpu.roll(jnp.broadcast_to(th[row, 0:1, :], (FZ, L)), 4 + 8 * 6, 1), acc)
        for f in range(F):
            g = 7 + f
            acc = jnp.where(group == g, pltpu.roll(jnp.broadcast_to(rg[f : f + 1, L : 2 * L], (FZ, L)), 4 + 8 * g, 1), acc)
        out[0:40, :] = acc
    acc = jnp.zeros((FZ, L), F32)
    for f in range(F):
        for h in range(2):
            g = f * 2 + h
            acc = jnp.where(group == g, pltpu.roll(ch[f, h * 40 : h * 40 + 40, :], (4 + 8 * g) % L, 1), acc)
    mca[40:80, :] = acc
    mcb[40:80, :] = acc


def ring_sum_diff(tiles_sum, tiles_diff, lane):
    def shifted(tiles):
        up = [pltpu.roll(t, L - 1, 1) for t in tiles]
        down = [pltpu.roll(t, 1, 1) for t in tiles]
        n = len(tiles)
        up = [jnp.where(lane < L - 1, up[t], up[(t + 1) % n]) for t in range(n)]
        down = [jnp.where(lane > 0, down[t], down[(t - 1) % n]) for t in range(n)]
        return up, down

    a, b = shifted(tiles_sum)
    c, d = shifted(tiles_diff)
    return [p + q for p, q in zip(a, b)], [p - q for p, q in zip(c, d)]


def vector_piece(load, own, nt, inv2j, invjj, h, lane):
    ia = 1.0 / (h * h)
    q = 0.25 * ia
    s = 0.5 / h
    cache = {}

    def u(i, r, t, dz=0):
        key = (i, r, t, dz)
        if key not in cache:
            cache[key] = load(i, r, t, dz)
        return cache[key]

    grads = {}

    def g(i, r, t):
        key = (i, r, t)
        if key not in grads:
            grads[key] = (u(i, r, t, 1) - u(i, r, t, -1)) * (inv2j(r, t) * s)
        return grads[key]

    out = {}
    ts = range(nt)
    for r in own:
        inner = (
            [q * (u(1, r + 1, t) - u(1, r - 1, t)) for t in ts],
            [q * (u(0, r + 1, t) - u(0, r - 1, t)) + g(2, r, t) for t in ts],
            [g(1, r, t) for t in ts],
        )
        for i in range(3):
            side, mixed = ring_sum_diff([u(i, r, t) for t in ts], inner[i], lane)
            for t in ts:
                c = u(i, r, t)
                c2 = c + c
                xx = (u(i, r + 1, t) + u(i, r - 1, t) - c2) * ia
                yy = (side[t] - c2) * ia
                zz = (u(i, r, t, 1) + u(i, r, t, -1) - c2) * invjj(r, t)
                cross = mixed[t]
                if i == 0:
                    cross = cross + (g(2, r + 1, t) - g(2, r - 1, t))
                if i == 2:
                    cross = cross + (g(0, r + 1, t) - g(0, r - 1, t))
                out[i, r, t] = (c2, xx + yy + zz, (xx, yy, zz)[i] + cross)
    return out


def interpolate(cc, spread, edges, lane8):
    left, right, low, high = edges
    a, b, c = cc[0], cc[1], cc[2]
    zero = jnp.zeros_like(a)
    mixes = [
        jnp.where(left, 0.75 * a + 0.25 * b, zero),
        0.75 * b + 0.25 * a,
        0.75 * b + 0.25 * c,
        jnp.where(right, 0.75 * c + 0.25 * b, zero),
    ]
    plane = exact_dot(jnp.concatenate(mixes, axis=0), spread[...])
    keep = (lane8 < 2 * L) | ((lane8 < 2 * L + 64) & high) | ((lane8 >= 2 * L + 64) & low)
    return jnp.where(keep, plane, 0.0)


def edges_here():
    x, y = lax.axis_index("gx"), lax.axis_index("gy")
    return x > 0, x < lax.axis_size("gx") - 1, y > 0, y < lax.axis_size("gy") - 1


def fill_ghosts(U, V, cc, spread, edges):
    for f in range(3):
        for r in range(3):
            for t in range(2):
                cc[r, f : f + 1, t * L : (t + 1) * L] = V[f, r, t, ZP : ZP + 1, :]
    plane = interpolate(cc, spread, edges, lanes((32, 384)))
    for f in range(3):
        for r in range(4):
            for t in range(3):
                U[f, r, t, ZP + FZ : ZP + FZ + 1, :] = plane[r * 8 + f : r * 8 + f + 1, t * L : (t + 1) * L]
                U[f, r, t, ZP - 1 : ZP, :] = U[f, r, t, ZP : ZP + 1, :]
        for r in range(3):
            for t in range(2):
                V[f, r, t, ZP + CZ : ZP + CZ + 1, :] = jnp.zeros((1, L), F32)


def one_field(kernel, a):
    def body(*refs):
        kernel(a, *refs)

    body.__name__ = kernel.__name__
    return body


def fine_pieces(U, jv, lane):
    for k in range(FZ // 8):
        at = ZP + 8 * k
        parts = vector_piece(
            lambda i, r, t, dz: U[i, r, t, at + dz : at + dz + 8, :], (1, 2), 3,
            lambda r, t: jv[0, r, t], lambda r, t: jv[1, r, t], 1.0, lane,
        )
        for (i, r, t), values in parts.items():
            yield k, i, r - 1, t, values


def coarse_pieces(V, lane):
    for k in range(CZ // 8):
        at = ZP + 8 * k
        parts = vector_piece(
            lambda i, r, t, dz: V[i, r, t, at + dz : at + dz + 8, :], (1,), 2,
            lambda r, t: 0.25, lambda r, t: 0.25, 2.0, lane,
        )
        for (i, r, t), values in parts.items():
            yield k, i, t, values


def step_one(
    a, fn, fo, cn, co, sf, lf, sc, lc, tp, fh, foh, sh, th, ch, coh, sch, rg, rxa, rxb, rca, rcb, spread, pool,
    f1, c1, c1h, rg1, mxa, mxb, jv, cf, cv, U, V, cc, tmp,
):
    px = lax.rem(lax.axis_index("gx"), 2)
    edges = edges_here()
    lane = lanes((8, L))
    lane40 = lanes((FZ, L))
    near40 = ((lane40 + 4) & 127) < 8

    def corner(rc, part, g):
        return jnp.where(near40, pltpu.roll(rc[part * 40 : part * 40 + 40, :], (2 * L - 4 - 8 * g) % L, 1), 0.0)

    cc[...] = jnp.zeros_like(cc)
    body = slice(ZP, ZP + FZ)
    for i in range(3):
        f = 3 * a + i
        for x in range(2):
            for t in range(2):
                U[i, 1 + x, t, body, :] = fn[fine_rows(f, t, x), :]
            U[i, 1 + x, 2, body, :] = fh[f * 2 + x]
        V[i, 1, 0, ZP : ZP + CZ, :] = cn[f * CZ : (f + 1) * CZ, :]
        V[i, 1, 1, ZP : ZP + CZ, :] = ch[f]
        for t in range(2):
            V[i, 1, t, ZP - 1 : ZP, :] = rg[f : f + 1, t * L : (t + 1) * L]
    for rx, rc, fr, cr in ((rxa.at[a * HALF : (a + 1) * HALF, :], rca, 3 * (1 - px), 2 * (1 - px)), (rxb, rcb, 3 * px, 2 * px)):
        for i in range(3):
            f = 3 * a + i
            for t in range(2):
                U[i, fr, t, body, :] = rx[i * 80 + t * 40 : i * 80 + t * 40 + 40, :]
            U[i, fr, 2, body, :] = corner(rc, 0, f)
            V[i, cr, 0, ZP : ZP + CZ, :] = rx[HCOARSE + i * CZ : HCOARSE + (i + 1) * CZ, :]
            for half in range(2):
                V[i, cr, 1, ZP + half * 40 : ZP + half * 40 + 40, :] = corner(rc, 1, f * 2 + half)
            V[i, cr, 0, ZP - 1 : ZP, :] = rx[HFINE + i : HFINE + i + 1, :]
            V[i, cr, 1, ZP - 1 : ZP, :] = corner(rc, 0, 7 + f)[0:1, :]
        for t in range(2):
            jv[0, fr, t] = jnp.broadcast_to(rx[HTOPO + t : HTOPO + t + 1, :], (8, L))
        jv[0, fr, 2] = corner(rc, 0, 6)[0:8, :]
    for x in range(2):
        for t in range(2):
            jv[0, 1 + x, t] = jnp.broadcast_to(tp[t * 2 + x : t * 2 + x + 1, :].astype(F32), (8, L))
        jv[0, 1 + x, 2] = th[x]
    for r in range(4):
        for t in range(3):
            spacing = 1.0 + jv[0, r, t] * (1.0 / 1024.0)
            jv[0, r, t] = 1.0 / (2.0 * spacing)
            jv[1, r, t] = 1.0 / (spacing * spacing)
    for x in range(2):
        for t in range(3):
            shear = sf[coef_rows(t, x), :] if t < 2 else sh[x]
            lame = lf[coef_rows(t, x), :] if t < 2 else sh[2 + x]
            cf[0, x, t] = DT2 * shear
            cf[1, x, t] = DT2 * (lame + shear)
    for t in range(2):
        shear = sc[...] if t == 0 else sch[0]
        lame = lc[...] if t == 0 else sch[1]
        cv[0, t] = DT2 * shear
        cv[1, t] = DT2 * (lame + shear)
    fill_ghosts(U, V, cc, spread, edges)
    keep = ((lane < 64) & edges[3]) | ((lane >= 64) & edges[2])
    for k, i, x, t, (c2, lap, gd) in fine_pieces(U, jv, lane):
        f = 3 * a + i
        zs = slice(8 * k, 8 * k + 8)
        old = fo[fine_rows(f, t, x, 8 * k, 8), :] if t < 2 else foh[f * 2 + x, zs, :]
        new = c2 - old + cf[0, x, t, zs, :] * lap + cf[1, x, t, zs, :] * gd
        f1[i * 2 + x, t, zs, :] = new if t < 2 else jnp.where(keep, new, 0.0)
    for k, i, t, (c2, lap, gd) in coarse_pieces(V, lane):
        f = 3 * a + i
        zs = slice(8 * k, 8 * k + 8)
        old = co[f * CZ + 8 * k : f * CZ + 8 * k + 8, :] if t == 0 else coh[f, zs, :]
        new = c2 - old + cv[0, t, zs, :] * lap + cv[1, t, zs, :] * gd
        if t == 0:
            c1[i * CZ + 8 * k : i * CZ + 8 * k + 8, :] = new
        else:
            c1h[i, zs, :] = jnp.where(keep, new, 0.0)
    tmp[...] = jnp.zeros_like(tmp)
    for i in range(3):
        for t in range(3):
            tmp[i : i + 1, t * L : (t + 1) * L] = f1[i * 2, t, FZ - 1 : FZ, :] + f1[i * 2 + 1, t, FZ - 1 : FZ, :]
    rg1[...] = exact_dot(tmp[...], pool[...])
    for out, row in ((mxb, px), (mxa, 1 - px)):
        for i in range(3):
            for t in range(2):
                out[i * 80 + t * 40 : i * 80 + t * 40 + 40, :] = f1[i * 2 + row, t]
        out[HFINE:HCOARSE, :] = rg1[:, 0:L]
        out[HCOARSE:HLATER, :] = later_corners(f1, c1h, row, lane40)
        out[HLATER : HLATER + 3 * CZ, :] = c1[...]
    mxb[HALF + 40 : HALF + 48, :] = jnp.zeros((8, L), F32)


def later_corners(f1, c1h, row, lane40):
    group = lane40 >> 2
    acc = jnp.zeros((FZ, L), F32)
    for i in range(3):
        acc = jnp.where(group == i, pltpu.roll(f1[i * 2 + row, 2], 2 + 4 * i, 1), acc)
        for half in range(2):
            g = 3 + 2 * i + half
            acc = jnp.where(group == g, pltpu.roll(c1h[i, half * 40 : half * 40 + 40, :], 2 + 4 * g, 1), acc)
    return acc


def step_two(a, fn, cn, f1, c1, c1h, rg1, rxa, rxb, jv, cf, cv, spread, fout, cout, U, V, cc, after_fine=None):
    px = lax.rem(lax.axis_index("gx"), 2)
    edges = edges_here()
    lane = lanes((8, L))
    near40 = ((lanes((FZ, L)) + 2) & 127) < 4

    def corner(rx, g):
        return jnp.where(near40, pltpu.roll(rx[HCOARSE:HLATER, :], (2 * L - 2 - 4 * g) % L, 1), 0.0)

    cc[...] = jnp.zeros_like(cc)
    body = slice(ZP, ZP + FZ)
    for i in range(3):
        for x in range(2):
            for t in range(3):
                U[i, 1 + x, t, body, :] = f1[i * 2 + x, t]
        V[i, 1, 0, ZP : ZP + CZ, :] = c1[i * CZ : (i + 1) * CZ, :]
        V[i, 1, 1, ZP : ZP + CZ, :] = c1h[i]
        for t in range(2):
            V[i, 1, t, ZP - 1 : ZP, :] = rg1[i : i + 1, t * L : (t + 1) * L]
    for rx, fr, cr in ((rxa, 3 * (1 - px), 2 * (1 - px)), (rxb, 3 * px, 2 * px)):
        for i in range(3):
            for t in range(2):
                U[i, fr, t, body, :] = rx[i * 80 + t * 40 : i * 80 + t * 40 + 40, :]
            U[i, fr, 2, body, :] = corner(rx, i)
            V[i, cr, 0, ZP : ZP + CZ, :] = rx[HLATER + i * CZ : HLATER + (i + 1) * CZ, :]
            for half in range(2):
                V[i, cr, 1, ZP + half * 40 : ZP + half * 40 + 40, :] = corner(rx, 3 + i * 2 + half)
            V[i, cr, 0, ZP - 1 : ZP, :] = rx[HFINE + i : HFINE + i + 1, :]
            V[i, cr, 1, ZP - 1 : ZP, :] = jnp.zeros((1, L), F32)
    fill_ghosts(U, V, cc, spread, edges)
    for k, i, x, t, (c2, lap, gd) in fine_pieces(U, jv, lane):
        if t < 2:
            zs = slice(8 * k, 8 * k + 8)
            old = fn[fine_rows(3 * a + i, t, x, 8 * k, 8), :]
            fout[fine_rows(i, t, x, 8 * k, 8), :] = c2 - old + cf[0, x, t, zs, :] * lap + cf[1, x, t, zs, :] * gd
    if after_fine is not None:
        after_fine()
    for k, i, t, (c2, lap, gd) in coarse_pieces(V, lane):
        if t == 0:
            zs = slice(8 * k, 8 * k + 8)
            f = 3 * a + i
            old = cn[f * CZ + 8 * k : f * CZ + 8 * k + 8, :]
            cout[i * CZ + 8 * k : i * CZ + 8 * k + 8, :] = c2 - old + cv[0, t, zs, :] * lap + cv[1, t, zs, :] * gd


def step_two_first(fn, cn, f1, c1, c1h, rg1, rxa, rxb, jv, cf, cv, spread, f1g, c1g, fout, cout, fk1, ck1, U, V, cc):
    step_two(0, fn, cn, f1, c1, c1h, rg1, rxa, rxb, jv, cf, cv, spread, fout, cout, U, V, cc)
    for q in range(4):
        x, t = q // 2, q % 2
        total = jnp.zeros((FZ, L), F32)
        for i in range(3):
            total = total + f1[i * 2 + x, t] * f1g[i * 2 + x, t]
        fk1[q] = total
    total = jnp.zeros((CZ, L), F32)
    for i in range(3):
        total = total + c1[i * CZ : (i + 1) * CZ, :] * c1g[i * CZ : (i + 1) * CZ, :]
    ck1[...] = total


def step_two_last(
    fn, cn, f1, c1, c1h, rg1, rxa, rxb, jv, cf, cv, spread, fof, cof, fk1, ck1,
    fout, cout, fk, ck, U, V, cc, fog, cog, fks, cks, sems,
):
    half_f, half_c = 3 * FZ * 4, 3 * CZ
    copies = [
        pltpu.make_async_copy(fof, fout.at[0:half_f, :], sems.at[0]),
        pltpu.make_async_copy(cof, cout.at[0:half_c, :], sems.at[1]),
        pltpu.make_async_copy(fog, fout.at[half_f : 2 * half_f, :], sems.at[2]),
        pltpu.make_async_copy(cog, cout.at[half_c : 2 * half_c, :], sems.at[3]),
        pltpu.make_async_copy(fks, fk, sems.at[4]),
        pltpu.make_async_copy(cks, ck, sems.at[5]),
    ]
    copies[0].start()
    copies[1].start()

    def fine_done():
        copies[2].start()

    step_two(1, fn, cn, f1, c1, c1h, rg1, rxa, rxb, jv, cf, cv, spread, fog, cog, U, V, cc, fine_done)
    copies[3].start()
    total = ck1[...]
    for i in range(3):
        total = total + cof[i * CZ : (i + 1) * CZ, :] * cog[i * CZ : (i + 1) * CZ, :]
    cks[...] = total
    copies[5].start()
    for x in range(2):
        for t in range(2):
            total = fk1[x * 2 + t]
            for i in range(3):
                total = total + fof[fine_rows(i, t, x), :] * fog[fine_rows(i, t, x), :]
            fks[coef_rows(t, x), :] = total
    copies[4].start()
    for copy in copies:
        copy.wait()


def call(kernel, args, outs, scratch, space=VM, megabytes=12, flops=0, out_space=VM):
    shapes = tuple(jax.ShapeDtypeStruct(s, F32) if isinstance(s, tuple) else s for s in outs)
    return pl.pallas_call(
        kernel,
        out_shape=shapes,
        in_specs=[space] * len(args),
        out_specs=(out_space,) * len(outs),
        scratch_shapes=[pltpu.VMEM(s, F32) if isinstance(s, tuple) else s for s in scratch],
        cost_estimate=pl.CostEstimate(flops=flops, transcendentals=0, bytes_accessed=1024) if flops else None,
        compiler_params=pltpu.CompilerParams(vmem_limit_bytes=megabytes * 1024 * 1024),
    )(*args)


def swap(cells, axis, first):
    count = lax.axis_size(axis)
    return lax.ppermute(cells, axis, [p for i in range(first, count - 1, 2) for p in ((i, i + 1), (i + 1, i))])


def rows_of(array):
    lead = array.size // 512
    return array.reshape(lead, 2, 2, L).transpose(0, 2, 1, 3).reshape(lead * 4, L)


def fine_of(rows, shape):
    return rows.reshape(-1, 2, 2, L).transpose(0, 2, 1, 3).reshape(shape)


def on_device(fine_old, fine_now, coarse_old, coarse_now, shear_fine, lame_fine, shear_coarse, lame_coarse, topography):
    fo, fn, sf, lf = rows_of(fine_old), rows_of(fine_now), rows_of(shear_fine), rows_of(lame_fine)
    tp = rows_of(topography)
    co, cn = coarse_old.reshape(-1, L), coarse_now.reshape(-1, L)
    sc, lc = shear_coarse.reshape(-1, L), lame_coarse.reshape(-1, L)
    pool, spread = jnp.asarray(POOL), jnp.asarray(SPREAD)
    raw = (fn, fo, cn, co, sf, lf, sc, lc, tp, pool, spread)
    raw = tuple(pltpu.with_memory_space_constraint(v, pltpu.HBM) for v in raw)
    local = call(
        load_and_pack_y,
        raw,
        tuple(jax.ShapeDtypeStruct(v.shape, v.dtype) for v in raw) + ((2 * HALF, L), (HALF + 8, L), (HALF + 8, L), (80, L), (80, L)),
        ((8, 256), pltpu.SemaphoreType.DMA((len(raw),)),),
        pl.BlockSpec(memory_space=pltpu.HBM),
    )
    fn, fo, cn, co, sf, lf, sc, lc, tp, pool, spread, ma, mbf, mbg, mya, myb = local
    ryb = swap(myb, "gy", 1)
    rya = swap(mya, "gy", 0)
    by_link = [swap(m, "gx", 1) for m in (mbf, mbg)]
    in_chip = swap(ma, "gx", 0)
    fh, foh, sh, th, ch, coh, sch, rg, mca, mcb = call(
        open_y,
        (ryb, rya, fn, pool),
        ((12, FZ, L), (12, FZ, L), (4, FZ, L), (2, 8, L), (F, CZ, L), (F, CZ, L), (2, CZ, L), (8, 256), (80, L), (80, L)),
        ((8, 384),),
        flops=C_OPEN,
    )
    rcb = swap(mcb, "gx", 1)
    rca = swap(mca, "gx", 0)
    field = ((3, 4, 3, 56, L), (3, 3, 2, 96, L), (3, 8, 256))
    firsts, far, near = [], [], []
    for a in range(2):
        *results, mxa, mxb, jv, cf, cv = call(
            one_field(step_one, a),
            (fn, fo, cn, co, sf, lf, sc, lc, tp, fh, foh, sh, th, ch, coh, sch, rg, in_chip, by_link[a], rca, rcb, spread, pool),
            ((6, 3, FZ, L), (3 * CZ, L), (3, CZ, L), (8, 256), (HALF + 40, L), (HALF + 48, L), (2, 4, 3, 8, L), (2, 2, 3, FZ, L), (2, 2, CZ, L)),
            field + ((8, 384),),
            flops=C_ONE[a],
        )
        firsts.append(results)
        far.append(swap(mxb, "gx", 1))
        near.append(swap(mxa, "gx", 0))
    fof, cof, fk1, ck1 = call(
        step_two_first,
        (fn, cn, *firsts[0], near[0], far[0], jv, cf, cv, spread, *firsts[1][:2]),
        ((3 * FZ * 4, L), (3 * CZ, L), (4, FZ, L), (CZ, L)),
        field,
        flops=C_TWO,
    )
    fout, cout, fk, ck = call(
        step_two_last,
        (fn, cn, *firsts[1], near[1], far[1], jv, cf, cv, spread, fof, cof, fk1, ck1),
        ((FINE_ROWS, L), (COARSE_ROWS, L), (4 * FZ, L), (CZ, L)),
        field + ((3 * FZ * 4, L), (3 * CZ, L), (4 * FZ, L), (CZ, L), pltpu.SemaphoreType.DMA((6,))),
        out_space=pl.BlockSpec(memory_space=pltpu.HBM),
    )
    return (
        fine_of(fout, fine_now.shape),
        cout.reshape(coarse_now.shape),
        fine_of(fk, shear_fine.shape),
        ck.reshape(shear_coarse.shape),
    )


def solution(mesh):
    fields = P(None, None, None, "gx", "gy")
    cells = P(None, "gx", "gy")
    return jax.shard_map(
        on_device,
        mesh=mesh,
        in_specs=(fields, fields, fields, fields, cells, cells, cells, cells, P("gx", "gy")),
        out_specs=(fields, fields, cells, cells),
        check_vma=False,
    )
```

```python
import jax
import jax.numpy as jnp
import ml_dtypes
import numpy as np
from jax import lax
from jax.experimental import pallas as pl
from jax.experimental.pallas import tpu as pltpu
from jax.sharding import PartitionSpec as P

F = 6
FZ = 40
CZ = 80
L = 128
ZP = 8
DT2 = 0.04
F32 = jnp.float32

FINE_ROWS = F * FZ * 4
COARSE_ROWS = F * CZ
HFINE = 3 * 2 * FZ
HTOPO = HFINE + 3
HCOARSE = HFINE + 8
HALF = HCOARSE + 3 * CZ
CORNERS = 16
HLATER = HCOARSE + CORNERS
C_OPEN = 4*10**9
C_ONE = (4*10**9, 10**9)
C_TWO = 1
VM = pl.BlockSpec(memory_space=pltpu.VMEM)


def pool_weights():
    w = np.zeros((384, 256), np.float32)
    for n in range(384):
        if n < 256:
            w[n, n // 2] = 0.25
        else:
            k = n - 256
            w[n, 128 + (k // 2 if k < 64 else 64 + k // 2)] = 0.25
    return w.astype(ml_dtypes.bfloat16)


def spread_weights():
    w = np.zeros((256, 384), np.float32)
    for n in range(384):
        col = n if n < 320 else n - 384
        j = col // 2
        w[j % 256, n] += 0.75
        w[(j + (1 if col % 2 else -1)) % 256, n] += 0.25
    return w.astype(ml_dtypes.bfloat16)


POOL = pool_weights()
SPREAD = spread_weights()


def exact_dot(rows, weights):
    hi = rows.astype(jnp.bfloat16)
    rest = rows - hi.astype(F32)
    mid = rest.astype(jnp.bfloat16)
    low = (rest - mid.astype(F32)).astype(jnp.bfloat16)
    dot = lambda part: jnp.dot(part, weights, preferred_element_type=F32)
    return dot(hi) + (dot(mid) + dot(low))


def lanes(shape):
    return lax.broadcasted_iota(jnp.int32, shape, len(shape) - 1)


def fine_rows(f, lt, x, start=0, size=FZ):
    return pl.ds((f * FZ + start) * 4 + lt * 2 + x, size, stride=4)


def coef_rows(lt, x, start=0, size=FZ):
    return pl.ds(start * 4 + lt * 2 + x, size, stride=4)


def load_and_pack_y(*refs):
    n = 11
    hbm, (fn, fo, cn, co, sf, lf, sc, lc, tp, pool, spread), (ma, mbf, mbg, mya, myb, tmp, sems) = refs[:n], refs[n : 2 * n], refs[2 * n :]
    copies = [pltpu.make_async_copy(src, dst, sems.at[q]) for q, (src, dst) in enumerate(zip(hbm, refs[n : 2 * n]))]
    early = (0, 2, 8, 9)
    late = [q for q in range(n) if q not in early]
    for q in (*early, *late):
        copies[q].start()
    for q in early:
        copies[q].wait()
    pack_x(fn, cn, tp, pool, (ma, mbf, mbg), tmp)
    for q in late:
        copies[q].wait()
    py = lax.rem(lax.axis_index("gy"), 2)
    group = lanes((FZ, L)) >> 2
    for out, right in ((mya, 1 - py), (myb, py)):
        base = 4 * right
        acc = jnp.zeros((FZ, L), F32)
        for arr, at in ((fn, 0), (fo, 12)):
            for f in range(F):
                for x in range(2):
                    g = at + f * 2 + x
                    acc = jnp.where(group == g, pltpu.roll(arr[fine_rows(f, right, x), :], lax.rem(base + 4 * g, L), 1), acc)
        for arr, at in ((sf, 24), (lf, 26)):
            for x in range(2):
                g = at + x
                acc = jnp.where(group == g, pltpu.roll(arr[coef_rows(right, x), :], lax.rem(base + 4 * g, L), 1), acc)
        for x in range(2):
            g = 28 + x
            plane = jnp.broadcast_to(tp[pl.ds(right * 2 + x, 1), :].astype(F32), (FZ, L))
            acc = jnp.where(group == g, pltpu.roll(plane, lax.rem(base + 4 * g, L), 1), acc)
        out[0:40, :] = acc
        acc = jnp.zeros((FZ, L), F32)
        for arr, at, count in ((cn, 0, F), (co, 12, F), (sc, 24, 1), (lc, 26, 1)):
            for f in range(count):
                for h in range(2):
                    g = at + f * 2 + h
                    acc = jnp.where(group == g, pltpu.roll(arr[f * CZ + h * 40 : f * CZ + h * 40 + 40, :], lax.rem(base + 4 * g, L), 1), acc)
        out[40:80, :] = acc


def bottom_sums(fn, tmp):
    for f in range(F):
        for lt in range(2):
            at = (f * FZ + FZ - 1) * 4 + lt * 2
            tmp[f : f + 1, lt * L : (lt + 1) * L] = fn[at : at + 1, :] + fn[at + 1 : at + 2, :]


def pack_x(fn, cn, tp, pool, outs, tmp):
    px = lax.rem(lax.axis_index("gx"), 2)
    tmp[...] = jnp.zeros_like(tmp)
    bottom_sums(fn, tmp)
    ridge = exact_dot(tmp[...], pool[0:256, 0:L])
    ma, mbf, mbg = outs
    in_chip = (ma.at[0:HALF, :], ma.at[HALF : 2 * HALF, :])
    for out, a, row in zip((*in_chip, mbf, mbg), (0, 1, 0, 1), (1 - px, 1 - px, px, px)):
        for i in range(3):
            for lt in range(2):
                out[i * 80 + lt * 40 : i * 80 + lt * 40 + 40, :] = fn[fine_rows(a * 3 + i, lt, row), :]
        out[HFINE : HFINE + 3, :] = ridge[a * 3 : a * 3 + 3, :]
        for lt in range(2):
            out[HTOPO + lt : HTOPO + lt + 1, :] = tp[pl.ds(lt * 2 + row, 1), :].astype(F32)
        out[HTOPO + 2 : HCOARSE, :] = jnp.zeros((3, L), F32)
        out[HCOARSE : HCOARSE + 3 * CZ, :] = cn[a * 3 * CZ : (a + 1) * 3 * CZ, :]


def open_y(ryb, rya, fn, pool, fh, foh, sh, th, ch, coh, sch, rg, mca, mcb, tmp):
    px = lax.rem(lax.axis_index("gx"), 2)
    py = lax.rem(lax.axis_index("gy"), 2)
    lane = lanes((FZ, L))
    in_a = ((lane + 4 * py) & 127) < 4
    in_b = ((lane + 4 * (1 - py)) & 127) < 4

    def halo(g, part):
        a = pltpu.roll(rya[part * 40 : part * 40 + 40, :], lax.rem(256 - 4 * g - 4 * py, L), 1)
        b = pltpu.roll(ryb[part * 40 : part * 40 + 40, :], lax.rem(256 - 4 * g - 4 * (1 - py), L), 1)
        return jnp.where(in_a, a, jnp.where(in_b, b, 0.0))

    for q in range(12):
        fh[q] = halo(q, 0)
        foh[q] = halo(12 + q, 0)
    for q in range(4):
        sh[q] = halo(24 + q, 0)
    for x in range(2):
        th[x] = halo(28 + x, 0)[0:8, :]
    for f in range(F):
        for h in range(2):
            ch[f, h * 40 : h * 40 + 40, :] = halo(f * 2 + h, 1)
            coh[f, h * 40 : h * 40 + 40, :] = halo(12 + f * 2 + h, 1)
    for q in range(2):
        for h in range(2):
            sch[q, h * 40 : h * 40 + 40, :] = halo(24 + q * 2 + h, 1)
    tmp[...] = jnp.zeros_like(tmp)
    bottom_sums(fn, tmp)
    for f in range(F):
        tmp[f : f + 1, 2 * L : 3 * L] = fh[f * 2, 39:40, :] + fh[f * 2 + 1, 39:40, :]
    rg[...] = exact_dot(tmp[...], pool[...])
    group = lane >> 3
    for out, row in ((mca, 1 - px), (mcb, px)):
        acc = jnp.zeros((FZ, L), F32)
        for f in range(F):
            acc = jnp.where(group == f, pltpu.roll(fh[f * 2 + row], 4 + 8 * f, 1), acc)
        acc = jnp.where(group == 6, pltpu.roll(jnp.broadcast_to(th[row, 0:1, :], (FZ, L)), 4 + 8 * 6, 1), acc)
        for f in range(F):
            g = 7 + f
            acc = jnp.where(group == g, pltpu.roll(jnp.broadcast_to(rg[f : f + 1, L : 2 * L], (FZ, L)), 4 + 8 * g, 1), acc)
        out[0:40, :] = acc
    acc = jnp.zeros((FZ, L), F32)
    for f in range(F):
        for h in range(2):
            g = f * 2 + h
            acc = jnp.where(group == g, pltpu.roll(ch[f, h * 40 : h * 40 + 40, :], (4 + 8 * g) % L, 1), acc)
    mca[40:80, :] = acc
    mcb[40:80, :] = acc


def ring_sum_diff(tiles_sum, tiles_diff, lane):
    def shifted(tiles):
        up = [pltpu.roll(t, L - 1, 1) for t in tiles]
        down = [pltpu.roll(t, 1, 1) for t in tiles]
        n = len(tiles)
        up = [jnp.where(lane < L - 1, up[t], up[(t + 1) % n]) for t in range(n)]
        down = [jnp.where(lane > 0, down[t], down[(t - 1) % n]) for t in range(n)]
        return up, down

    a, b = shifted(tiles_sum)
    c, d = shifted(tiles_diff)
    return [p + q for p, q in zip(a, b)], [p - q for p, q in zip(c, d)]


def vector_piece(load, own, nt, inv2j, invjj, h, lane):
    ia = 1.0 / (h * h)
    q = 0.25 * ia
    s = 0.5 / h
    cache = {}

    def u(i, r, t, dz=0):
        key = (i, r, t, dz)
        if key not in cache:
            cache[key] = load(i, r, t, dz)
        return cache[key]

    grads = {}

    def g(i, r, t):
        key = (i, r, t)
        if key not in grads:
            grads[key] = (u(i, r, t, 1) - u(i, r, t, -1)) * (inv2j(r, t) * s)
        return grads[key]

    out = {}
    ts = range(nt)
    for r in own:
        inner = (
            [q * (u(1, r + 1, t) - u(1, r - 1, t)) for t in ts],
            [q * (u(0, r + 1, t) - u(0, r - 1, t)) + g(2, r, t) for t in ts],
            [g(1, r, t) for t in ts],
        )
        for i in range(3):
            side, mixed = ring_sum_diff([u(i, r, t) for t in ts], inner[i], lane)
            for t in ts:
                c = u(i, r, t)
                c2 = c + c
                xx = (u(i, r + 1, t) + u(i, r - 1, t) - c2) * ia
                yy = (side[t] - c2) * ia
                zz = (u(i, r, t, 1) + u(i, r, t, -1) - c2) * invjj(r, t)
                cross = mixed[t]
                if i == 0:
                    cross = cross + (g(2, r + 1, t) - g(2, r - 1, t))
                if i == 2:
                    cross = cross + (g(0, r + 1, t) - g(0, r - 1, t))
                out[i, r, t] = (c2, xx + yy + zz, (xx, yy, zz)[i] + cross)
    return out


def interpolate(cc, spread, edges, lane8):
    left, right, low, high = edges
    a, b, c = cc[0], cc[1], cc[2]
    zero = jnp.zeros_like(a)
    mixes = [
        jnp.where(left, 0.75 * a + 0.25 * b, zero),
        0.75 * b + 0.25 * a,
        0.75 * b + 0.25 * c,
        jnp.where(right, 0.75 * c + 0.25 * b, zero),
    ]
    plane = exact_dot(jnp.concatenate(mixes, axis=0), spread[...])
    keep = (lane8 < 2 * L) | ((lane8 < 2 * L + 64) & high) | ((lane8 >= 2 * L + 64) & low)
    return jnp.where(keep, plane, 0.0)


def edges_here():
    x, y = lax.axis_index("gx"), lax.axis_index("gy")
    return x > 0, x < lax.axis_size("gx") - 1, y > 0, y < lax.axis_size("gy") - 1


def fill_ghosts(U, V, cc, spread, edges):
    for f in range(3):
        for r in range(3):
            for t in range(2):
                cc[r, f : f + 1, t * L : (t + 1) * L] = V[f, r, t, ZP : ZP + 1, :]
    plane = interpolate(cc, spread, edges, lanes((32, 384)))
    for f in range(3):
        for r in range(4):
            for t in range(3):
                U[f, r, t, ZP + FZ : ZP + FZ + 1, :] = plane[r * 8 + f : r * 8 + f + 1, t * L : (t + 1) * L]
                U[f, r, t, ZP - 1 : ZP, :] = U[f, r, t, ZP : ZP + 1, :]
        for r in range(3):
            for t in range(2):
                V[f, r, t, ZP + CZ : ZP + CZ + 1, :] = jnp.zeros((1, L), F32)


def one_field(kernel, a):
    def body(*refs):
        kernel(a, *refs)

    body.__name__ = kernel.__name__
    return body


def fine_pieces(U, jv, lane):
    for k in range(FZ // 8):
        at = ZP + 8 * k
        parts = vector_piece(
            lambda i, r, t, dz: U[i, r, t, at + dz : at + dz + 8, :], (1, 2), 3,
            lambda r, t: jv[0, r, t], lambda r, t: jv[1, r, t], 1.0, lane,
        )
        for (i, r, t), values in parts.items():
            yield k, i, r - 1, t, values


def coarse_pieces(V, lane):
    for k in range(CZ // 8):
        at = ZP + 8 * k
        parts = vector_piece(
            lambda i, r, t, dz: V[i, r, t, at + dz : at + dz + 8, :], (1,), 2,
            lambda r, t: 0.25, lambda r, t: 0.25, 2.0, lane,
        )
        for (i, r, t), values in parts.items():
            yield k, i, t, values


def tables(tp, th, sf, lf, sc, lc, sh, sch, jv, cf, cv):
    for x in range(2):
        for t in range(2):
            jv[0, 1 + x, t] = jnp.broadcast_to(tp[t * 2 + x : t * 2 + x + 1, :].astype(F32), (8, L))
        jv[0, 1 + x, 2] = th[x]
    for r in range(4):
        for t in range(3):
            spacing = 1.0 + jv[0, r, t] * (1.0 / 1024.0)
            jv[0, r, t] = 1.0 / (2.0 * spacing)
            jv[1, r, t] = 1.0 / (spacing * spacing)
    for x in range(2):
        for t in range(3):
            shear = sf[coef_rows(t, x), :] if t < 2 else sh[x]
            lame = lf[coef_rows(t, x), :] if t < 2 else sh[2 + x]
            cf[0, x, t] = DT2 * shear
            cf[1, x, t] = DT2 * (lame + shear)
    for t in range(2):
        shear = sc[...] if t == 0 else sch[0]
        lame = lc[...] if t == 0 else sch[1]
        cv[0, t] = DT2 * shear
        cv[1, t] = DT2 * (lame + shear)


def step_one(
    a, fn, fo, cn, co, sf, lf, sc, lc, tp, fh, foh, sh, th, ch, coh, sch, rg, rxa, rxb, rca, rcb, spread, pool,
    f1, c1, c1h, rg1, mxa, mxb, jv, cf, cv, U, V, cc, tmp,
):
    px = lax.rem(lax.axis_index("gx"), 2)
    edges = edges_here()
    lane = lanes((8, L))
    lane40 = lanes((FZ, L))
    near40 = ((lane40 + 4) & 127) < 8

    def corner(rc, part, g):
        return jnp.where(near40, pltpu.roll(rc[part * 40 : part * 40 + 40, :], (2 * L - 4 - 8 * g) % L, 1), 0.0)

    cc[...] = jnp.zeros_like(cc)
    body = slice(ZP, ZP + FZ)
    for i in range(3):
        f = 3 * a + i
        for x in range(2):
            for t in range(2):
                U[i, 1 + x, t, body, :] = fn[fine_rows(f, t, x), :]
            U[i, 1 + x, 2, body, :] = fh[f * 2 + x]
        V[i, 1, 0, ZP : ZP + CZ, :] = cn[f * CZ : (f + 1) * CZ, :]
        V[i, 1, 1, ZP : ZP + CZ, :] = ch[f]
        for t in range(2):
            V[i, 1, t, ZP - 1 : ZP, :] = rg[f : f + 1, t * L : (t + 1) * L]
    for rx, rc, fr, cr in ((rxa.at[a * HALF : (a + 1) * HALF, :], rca, 3 * (1 - px), 2 * (1 - px)), (rxb, rcb, 3 * px, 2 * px)):
        for i in range(3):
            f = 3 * a + i
            for t in range(2):
                U[i, fr, t, body, :] = rx[i * 80 + t * 40 : i * 80 + t * 40 + 40, :]
            U[i, fr, 2, body, :] = corner(rc, 0, f)
            V[i, cr, 0, ZP : ZP + CZ, :] = rx[HCOARSE + i * CZ : HCOARSE + (i + 1) * CZ, :]
            for half in range(2):
                V[i, cr, 1, ZP + half * 40 : ZP + half * 40 + 40, :] = corner(rc, 1, f * 2 + half)
            V[i, cr, 0, ZP - 1 : ZP, :] = rx[HFINE + i : HFINE + i + 1, :]
            V[i, cr, 1, ZP - 1 : ZP, :] = corner(rc, 0, 7 + f)[0:1, :]
        if a == 0:
            for t in range(2):
                jv[0, fr, t] = jnp.broadcast_to(rx[HTOPO + t : HTOPO + t + 1, :], (8, L))
            jv[0, fr, 2] = corner(rc, 0, 6)[0:8, :]
    if a == 0:
        tables(tp, th, sf, lf, sc, lc, sh, sch, jv, cf, cv)
    fill_ghosts(U, V, cc, spread, edges)
    keep = ((lane < 64) & edges[3]) | ((lane >= 64) & edges[2])
    for k, i, x, t, (c2, lap, gd) in fine_pieces(U, jv, lane):
        f = 3 * a + i
        zs = slice(8 * k, 8 * k + 8)
        old = fo[fine_rows(f, t, x, 8 * k, 8), :] if t < 2 else foh[f * 2 + x, zs, :]
        new = c2 - old + cf[0, x, t, zs, :] * lap + cf[1, x, t, zs, :] * gd
        f1[i * 2 + x, t, zs, :] = new if t < 2 else jnp.where(keep, new, 0.0)
    for k, i, t, (c2, lap, gd) in coarse_pieces(V, lane):
        f = 3 * a + i
        zs = slice(8 * k, 8 * k + 8)
        old = co[f * CZ + 8 * k : f * CZ + 8 * k + 8, :] if t == 0 else coh[f, zs, :]
        new = c2 - old + cv[0, t, zs, :] * lap + cv[1, t, zs, :] * gd
        if t == 0:
            c1[i * CZ + 8 * k : i * CZ + 8 * k + 8, :] = new
        else:
            c1h[i, zs, :] = jnp.where(keep, new, 0.0)
    tmp[...] = jnp.zeros_like(tmp)
    for i in range(3):
        for t in range(3):
            tmp[i : i + 1, t * L : (t + 1) * L] = f1[i * 2, t, FZ - 1 : FZ, :] + f1[i * 2 + 1, t, FZ - 1 : FZ, :]
    rg1[...] = exact_dot(tmp[...], pool[...])
    for out, row in ((mxb, px), (mxa, 1 - px)):
        for i in range(3):
            for t in range(2):
                out[i * 80 + t * 40 : i * 80 + t * 40 + 40, :] = f1[i * 2 + row, t]
        out[HFINE:HCOARSE, :] = rg1[:, 0:L]
        out[HCOARSE:HLATER, :] = later_corners(f1, c1h, row, lane40)
        out[HLATER : HLATER + 3 * CZ, :] = c1[...]
    mxb[HALF + CORNERS : HALF + CORNERS + 8, :] = jnp.zeros((8, L), F32)


def step_one_adjoint(*refs):
    step_one(1, *refs[:23], *refs[26:32], *refs[23:26], *refs[32:])


def corner_group(k, g):
    return 4 * (9 * (k // 2) + g)


def later_corners(f1, c1h, row, lane40):
    group = lanes((8, L)) >> 2
    accs = [jnp.zeros((8, L), F32), jnp.zeros((8, L), F32)]
    for k in range(FZ // 8):
        zs = slice(8 * k, 8 * k + 8)
        for i in range(3):
            pieces = [(i, f1[i * 2 + row, 2, zs, :])]
            pieces += [(3 + 2 * i + half, c1h[i, half * 40 + 8 * k : half * 40 + 8 * k + 8, :]) for half in range(2)]
            for g, piece in pieces:
                at = corner_group(k, g)
                accs[k % 2] = jnp.where(group == at // 4, pltpu.roll(piece, (2 + at) % L, 1), accs[k % 2])
    return jnp.concatenate(accs, axis=0)


def step_two(a, fn, cn, f1, c1, c1h, rg1, rxa, rxb, jv, cf, cv, spread, fout, cout, U, V, cc, after_fine=None):
    px = lax.rem(lax.axis_index("gx"), 2)
    edges = edges_here()
    lane = lanes((8, L))
    near8 = ((lane + 2) & 127) < 4

    def corner(rx, g):
        pieces = []
        for k in range(FZ // 8):
            rows = rx[HCOARSE + 8 * (k % 2) : HCOARSE + 8 * (k % 2) + 8, :]
            pieces.append(jnp.where(near8, pltpu.roll(rows, (2 * L - 2 - corner_group(k, g)) % L, 1), 0.0))
        return jnp.concatenate(pieces, axis=0)

    cc[...] = jnp.zeros_like(cc)
    body = slice(ZP, ZP + FZ)
    for i in range(3):
        for x in range(2):
            for t in range(3):
                U[i, 1 + x, t, body, :] = f1[i * 2 + x, t]
        V[i, 1, 0, ZP : ZP + CZ, :] = c1[i * CZ : (i + 1) * CZ, :]
        V[i, 1, 1, ZP : ZP + CZ, :] = c1h[i]
        for t in range(2):
            V[i, 1, t, ZP - 1 : ZP, :] = rg1[i : i + 1, t * L : (t + 1) * L]
    for rx, fr, cr in ((rxa, 3 * (1 - px), 2 * (1 - px)), (rxb, 3 * px, 2 * px)):
        for i in range(3):
            for t in range(2):
                U[i, fr, t, body, :] = rx[i * 80 + t * 40 : i * 80 + t * 40 + 40, :]
            U[i, fr, 2, body, :] = corner(rx, i)
            V[i, cr, 0, ZP : ZP + CZ, :] = rx[HLATER + i * CZ : HLATER + (i + 1) * CZ, :]
            for half in range(2):
                V[i, cr, 1, ZP + half * 40 : ZP + half * 40 + 40, :] = corner(rx, 3 + i * 2 + half)
            V[i, cr, 0, ZP - 1 : ZP, :] = rx[HFINE + i : HFINE + i + 1, :]
            V[i, cr, 1, ZP - 1 : ZP, :] = jnp.zeros((1, L), F32)
    fill_ghosts(U, V, cc, spread, edges)
    for k, i, x, t, (c2, lap, gd) in fine_pieces(U, jv, lane):
        if t < 2:
            zs = slice(8 * k, 8 * k + 8)
            old = fn[fine_rows(3 * a + i, t, x, 8 * k, 8), :]
            fout[fine_rows(i, t, x, 8 * k, 8), :] = c2 - old + cf[0, x, t, zs, :] * lap + cf[1, x, t, zs, :] * gd
    if after_fine is not None:
        after_fine()
    for k, i, t, (c2, lap, gd) in coarse_pieces(V, lane):
        if t == 0:
            zs = slice(8 * k, 8 * k + 8)
            f = 3 * a + i
            old = cn[f * CZ + 8 * k : f * CZ + 8 * k + 8, :]
            cout[i * CZ + 8 * k : i * CZ + 8 * k + 8, :] = c2 - old + cv[0, t, zs, :] * lap + cv[1, t, zs, :] * gd


def step_two_first(fn, cn, f1, c1, c1h, rg1, rxa, rxb, jv, cf, cv, spread, f1g, c1g, fout, cout, fk1, ck1, U, V, cc):
    step_two(0, fn, cn, f1, c1, c1h, rg1, rxa, rxb, jv, cf, cv, spread, fout, cout, U, V, cc)
    for q in range(4):
        x, t = q // 2, q % 2
        total = jnp.zeros((FZ, L), F32)
        for i in range(3):
            total = total + f1[i * 2 + x, t] * f1g[i * 2 + x, t]
        fk1[q] = total
    total = jnp.zeros((CZ, L), F32)
    for i in range(3):
        total = total + c1[i * CZ : (i + 1) * CZ, :] * c1g[i * CZ : (i + 1) * CZ, :]
    ck1[...] = total


def step_two_last(
    fn, cn, f1, c1, c1h, rg1, rxa, rxb, jv, cf, cv, spread, fof, cof, fk1, ck1,
    fout, cout, fk, ck, U, V, cc, fog, cog, fks, cks, sems,
):
    half_f, half_c = 3 * FZ * 4, 3 * CZ
    copies = [
        pltpu.make_async_copy(fof, fout.at[0:half_f, :], sems.at[0]),
        pltpu.make_async_copy(cof, cout.at[0:half_c, :], sems.at[1]),
        pltpu.make_async_copy(fog, fout.at[half_f : 2 * half_f, :], sems.at[2]),
        pltpu.make_async_copy(cog, cout.at[half_c : 2 * half_c, :], sems.at[3]),
        pltpu.make_async_copy(fks, fk, sems.at[4]),
        pltpu.make_async_copy(cks, ck, sems.at[5]),
    ]
    copies[0].start()
    copies[1].start()

    def fine_done():
        copies[2].start()

    step_two(1, fn, cn, f1, c1, c1h, rg1, rxa, rxb, jv, cf, cv, spread, fog, cog, U, V, cc, fine_done)
    copies[3].start()
    total = ck1[...]
    for i in range(3):
        total = total + cof[i * CZ : (i + 1) * CZ, :] * cog[i * CZ : (i + 1) * CZ, :]
    cks[...] = total
    copies[5].start()
    for x in range(2):
        for t in range(2):
            total = fk1[x * 2 + t]
            for i in range(3):
                total = total + fof[fine_rows(i, t, x), :] * fog[fine_rows(i, t, x), :]
            fks[coef_rows(t, x), :] = total
    copies[4].start()
    for copy in copies:
        copy.wait()


def call(kernel, args, outs, scratch, space=VM, megabytes=12, flops=0, out_space=VM):
    shapes = tuple(jax.ShapeDtypeStruct(s, F32) if isinstance(s, tuple) else s for s in outs)
    return pl.pallas_call(
        kernel,
        out_shape=shapes,
        in_specs=[space] * len(args),
        out_specs=(out_space,) * len(outs),
        scratch_shapes=[pltpu.VMEM(s, F32) if isinstance(s, tuple) else s for s in scratch],
        cost_estimate=pl.CostEstimate(flops=flops, transcendentals=0, bytes_accessed=1024) if flops else None,
        compiler_params=pltpu.CompilerParams(vmem_limit_bytes=megabytes * 1024 * 1024),
    )(*args)


def swap(cells, axis, first):
    count = lax.axis_size(axis)
    return lax.ppermute(cells, axis, [p for i in range(first, count - 1, 2) for p in ((i, i + 1), (i + 1, i))])


def rows_of(array):
    lead = array.size // 512
    return array.reshape(lead, 2, 2, L).transpose(0, 2, 1, 3).reshape(lead * 4, L)


def fine_of(rows, shape):
    return rows.reshape(-1, 2, 2, L).transpose(0, 2, 1, 3).reshape(shape)


def on_device(fine_old, fine_now, coarse_old, coarse_now, shear_fine, lame_fine, shear_coarse, lame_coarse, topography):
    fo, fn, sf, lf = rows_of(fine_old), rows_of(fine_now), rows_of(shear_fine), rows_of(lame_fine)
    tp = rows_of(topography)
    co, cn = coarse_old.reshape(-1, L), coarse_now.reshape(-1, L)
    sc, lc = shear_coarse.reshape(-1, L), lame_coarse.reshape(-1, L)
    pool, spread = jnp.asarray(POOL), jnp.asarray(SPREAD)
    raw = (fn, fo, cn, co, sf, lf, sc, lc, tp, pool, spread)
    raw = tuple(pltpu.with_memory_space_constraint(v, pltpu.HBM) for v in raw)
    local = call(
        load_and_pack_y,
        raw,
        tuple(jax.ShapeDtypeStruct(v.shape, v.dtype) for v in raw) + ((2 * HALF, L), (HALF, L), (HALF, L), (80, L), (80, L)),
        ((8, 256), pltpu.SemaphoreType.DMA((len(raw),)),),
        pl.BlockSpec(memory_space=pltpu.HBM),
    )
    fn, fo, cn, co, sf, lf, sc, lc, tp, pool, spread, ma, mbf, mbg, mya, myb = local
    ryb = swap(myb, "gy", 1)
    rya = swap(mya, "gy", 0)
    by_link = [swap(m, "gx", 1) for m in (mbf, mbg)]
    in_chip = swap(ma, "gx", 0)
    fh, foh, sh, th, ch, coh, sch, rg, mca, mcb = call(
        open_y,
        (ryb, rya, fn, pool),
        ((12, FZ, L), (12, FZ, L), (4, FZ, L), (2, 8, L), (F, CZ, L), (F, CZ, L), (2, CZ, L), (8, 256), (80, L), (80, L)),
        ((8, 384),),
        flops=C_OPEN,
    )
    rcb = swap(mcb, "gx", 1)
    rca = swap(mca, "gx", 0)
    field = ((3, 4, 3, 56, L), (3, 3, 2, 96, L), (3, 8, 256))
    firsts, far, near = [], [], []
    for a in range(2):
        args = (fn, fo, cn, co, sf, lf, sc, lc, tp, fh, foh, sh, th, ch, coh, sch, rg, in_chip, by_link[a], rca, rcb, spread, pool)
        outs = ((6, 3, FZ, L), (3 * CZ, L), (3, CZ, L), (8, 256), (HALF + CORNERS, L), (HALF + CORNERS + 8, L))
        if a == 0:
            kernel, outs = one_field(step_one, 0), outs + ((2, 4, 3, 8, L), (2, 2, 3, FZ, L), (2, 2, CZ, L))
        else:
            kernel, args = step_one_adjoint, args + (jv, cf, cv)
        results = call(kernel, args, outs, field + ((8, 384),), flops=C_ONE[a])
        if a == 0:
            jv, cf, cv = results[6:]
        mxa, mxb = results[4:6]
        results = results[:4]
        firsts.append(results)
        far.append(swap(mxb, "gx", 1))
        near.append(swap(mxa, "gx", 0))
    fof, cof, fk1, ck1 = call(
        step_two_first,
        (fn, cn, *firsts[0], near[0], far[0], jv, cf, cv, spread, *firsts[1][:2]),
        ((3 * FZ * 4, L), (3 * CZ, L), (4, FZ, L), (CZ, L)),
        field,
        flops=C_TWO,
    )
    fout, cout, fk, ck = call(
        step_two_last,
        (fn, cn, *firsts[1], near[1], far[1], jv, cf, cv, spread, fof, cof, fk1, ck1),
        ((FINE_ROWS, L), (COARSE_ROWS, L), (4 * FZ, L), (CZ, L)),
        field + ((3 * FZ * 4, L), (3 * CZ, L), (4 * FZ, L), (CZ, L), pltpu.SemaphoreType.DMA((6,))),
        out_space=pl.BlockSpec(memory_space=pltpu.HBM),
    )
    return (
        fine_of(fout, fine_now.shape),
        cout.reshape(coarse_now.shape),
        fine_of(fk, shear_fine.shape),
        ck.reshape(shear_coarse.shape),
    )


def solution(mesh):
    fields = P(None, None, None, "gx", "gy")
    cells = P(None, "gx", "gy")
    return jax.shard_map(
        on_device,
        mesh=mesh,
        in_specs=(fields, fields, fields, fields, cells, cells, cells, cells, P("gx", "gy")),
        out_specs=(fields, fields, cells, cells),
        check_vma=False,
    )
```

```python
import jax
import jax.numpy as jnp
import ml_dtypes
import numpy as np
from jax import lax
from jax.experimental import pallas as pl
from jax.experimental.pallas import tpu as pltpu
from jax.sharding import PartitionSpec as P

F = 6
FZ = 40
CZ = 80
L = 128
ZP = 8
DT2 = 0.04
F32 = jnp.float32

FINE_ROWS = F * FZ * 4
COARSE_ROWS = F * CZ
HFINE = 3 * 2 * FZ
HTOPO = HFINE + 3
HCOARSE = HFINE + 8
HALF = HCOARSE + 3 * CZ
HLATER = HCOARSE + 40
C_OPEN = 5*10**9
C_ONE = (5*10**9, 5*10**9)
C_TWO = 1
C_BOTH = 1
VM = pl.BlockSpec(memory_space=pltpu.VMEM)


def pool_weights():
    w = np.zeros((384, 256), np.float32)
    for n in range(384):
        if n < 256:
            w[n, n // 2] = 0.25
        else:
            k = n - 256
            w[n, 128 + (k // 2 if k < 64 else 64 + k // 2)] = 0.25
    return w.astype(ml_dtypes.bfloat16)


def spread_weights():
    w = np.zeros((256, 384), np.float32)
    for n in range(384):
        col = n if n < 320 else n - 384
        j = col // 2
        w[j % 256, n] += 0.75
        w[(j + (1 if col % 2 else -1)) % 256, n] += 0.25
    return w.astype(ml_dtypes.bfloat16)


POOL = pool_weights()
SPREAD = spread_weights()


def exact_dot(rows, weights):
    hi = rows.astype(jnp.bfloat16)
    rest = rows - hi.astype(F32)
    mid = rest.astype(jnp.bfloat16)
    low = (rest - mid.astype(F32)).astype(jnp.bfloat16)
    dot = lambda part: jnp.dot(part, weights, preferred_element_type=F32)
    return dot(hi) + (dot(mid) + dot(low))


def lanes(shape):
    return lax.broadcasted_iota(jnp.int32, shape, len(shape) - 1)


def fine_rows(f, lt, x, start=0, size=FZ):
    return pl.ds((f * FZ + start) * 4 + lt * 2 + x, size, stride=4)


def coef_rows(lt, x, start=0, size=FZ):
    return pl.ds(start * 4 + lt * 2 + x, size, stride=4)


def load_and_pack_y(*refs):
    n = 11
    hbm, (fn, fo, cn, co, sf, lf, sc, lc, tp, pool, spread), (ma, mbf, mbg, mya, myb, tmp, sems) = refs[:n], refs[n : 2 * n], refs[2 * n :]
    copies = [pltpu.make_async_copy(src, dst, sems.at[q]) for q, (src, dst) in enumerate(zip(hbm, refs[n : 2 * n]))]
    early = (0, 2, 8, 9)
    late = [q for q in range(n) if q not in early]
    for q in (*early, *late):
        copies[q].start()
    for q in early:
        copies[q].wait()
    pack_x(fn, cn, tp, pool, (ma, mbf, mbg), tmp)
    for q in late:
        copies[q].wait()
    py = lax.rem(lax.axis_index("gy"), 2)
    group = lanes((FZ, L)) >> 2
    for out, right in ((mya, 1 - py), (myb, py)):
        base = 4 * right
        acc = jnp.zeros((FZ, L), F32)
        for arr, at in ((fn, 0), (fo, 12)):
            for f in range(F):
                for x in range(2):
                    g = at + f * 2 + x
                    acc = jnp.where(group == g, pltpu.roll(arr[fine_rows(f, right, x), :], lax.rem(base + 4 * g, L), 1), acc)
        for arr, at in ((sf, 24), (lf, 26)):
            for x in range(2):
                g = at + x
                acc = jnp.where(group == g, pltpu.roll(arr[coef_rows(right, x), :], lax.rem(base + 4 * g, L), 1), acc)
        for x in range(2):
            g = 28 + x
            plane = jnp.broadcast_to(tp[pl.ds(right * 2 + x, 1), :].astype(F32), (FZ, L))
            acc = jnp.where(group == g, pltpu.roll(plane, lax.rem(base + 4 * g, L), 1), acc)
        out[0:40, :] = acc
        acc = jnp.zeros((FZ, L), F32)
        for arr, at, count in ((cn, 0, F), (co, 12, F), (sc, 24, 1), (lc, 26, 1)):
            for f in range(count):
                for h in range(2):
                    g = at + f * 2 + h
                    acc = jnp.where(group == g, pltpu.roll(arr[f * CZ + h * 40 : f * CZ + h * 40 + 40, :], lax.rem(base + 4 * g, L), 1), acc)
        out[40:80, :] = acc


def bottom_sums(fn, tmp):
    for f in range(F):
        for lt in range(2):
            at = (f * FZ + FZ - 1) * 4 + lt * 2
            tmp[f : f + 1, lt * L : (lt + 1) * L] = fn[at : at + 1, :] + fn[at + 1 : at + 2, :]


def pack_x(fn, cn, tp, pool, outs, tmp):
    px = lax.rem(lax.axis_index("gx"), 2)
    tmp[...] = jnp.zeros_like(tmp)
    bottom_sums(fn, tmp)
    ridge = exact_dot(tmp[...], pool[0:256, 0:L])
    ma, mbf, mbg = outs
    in_chip = (ma.at[0:HALF, :], ma.at[HALF : 2 * HALF, :])
    for out, a, row in zip((*in_chip, mbf, mbg), (0, 1, 0, 1), (1 - px, 1 - px, px, px)):
        for i in range(3):
            for lt in range(2):
                out[i * 80 + lt * 40 : i * 80 + lt * 40 + 40, :] = fn[fine_rows(a * 3 + i, lt, row), :]
        out[HFINE : HFINE + 3, :] = ridge[a * 3 : a * 3 + 3, :]
        for lt in range(2):
            out[HTOPO + lt : HTOPO + lt + 1, :] = tp[pl.ds(lt * 2 + row, 1), :].astype(F32)
        out[HTOPO + 2 : HCOARSE, :] = jnp.zeros((3, L), F32)
        out[HCOARSE : HCOARSE + 3 * CZ, :] = cn[a * 3 * CZ : (a + 1) * 3 * CZ, :]
        if out.shape[0] > HALF:
            out[HALF : HALF + 8, :] = jnp.zeros((8, L), F32)


def open_y(ryb, rya, fn, pool, fh, foh, sh, th, ch, coh, sch, rg, mca, mcb, tmp):
    px = lax.rem(lax.axis_index("gx"), 2)
    py = lax.rem(lax.axis_index("gy"), 2)
    lane = lanes((FZ, L))
    in_a = ((lane + 4 * py) & 127) < 4
    in_b = ((lane + 4 * (1 - py)) & 127) < 4

    def halo(g, part):
        a = pltpu.roll(rya[part * 40 : part * 40 + 40, :], lax.rem(256 - 4 * g - 4 * py, L), 1)
        b = pltpu.roll(ryb[part * 40 : part * 40 + 40, :], lax.rem(256 - 4 * g - 4 * (1 - py), L), 1)
        return jnp.where(in_a, a, jnp.where(in_b, b, 0.0))

    for q in range(12):
        fh[q] = halo(q, 0)
        foh[q] = halo(12 + q, 0)
    for q in range(4):
        sh[q] = halo(24 + q, 0)
    for x in range(2):
        th[x] = halo(28 + x, 0)[0:8, :]
    for f in range(F):
        for h in range(2):
            ch[f, h * 40 : h * 40 + 40, :] = halo(f * 2 + h, 1)
            coh[f, h * 40 : h * 40 + 40, :] = halo(12 + f * 2 + h, 1)
    for q in range(2):
        for h in range(2):
            sch[q, h * 40 : h * 40 + 40, :] = halo(24 + q * 2 + h, 1)
    tmp[...] = jnp.zeros_like(tmp)
    bottom_sums(fn, tmp)
    for f in range(F):
        tmp[f : f + 1, 2 * L : 3 * L] = fh[f * 2, 39:40, :] + fh[f * 2 + 1, 39:40, :]
    rg[...] = exact_dot(tmp[...], pool[...])
    group = lane >> 3
    for out, row in ((mca, 1 - px), (mcb, px)):
        acc = jnp.zeros((FZ, L), F32)
        for f in range(F):
            acc = jnp.where(group == f, pltpu.roll(fh[f * 2 + row], 4 + 8 * f, 1), acc)
        acc = jnp.where(group == 6, pltpu.roll(jnp.broadcast_to(th[row, 0:1, :], (FZ, L)), 4 + 8 * 6, 1), acc)
        for f in range(F):
            g = 7 + f
            acc = jnp.where(group == g, pltpu.roll(jnp.broadcast_to(rg[f : f + 1, L : 2 * L], (FZ, L)), 4 + 8 * g, 1), acc)
        out[0:40, :] = acc
    acc = jnp.zeros((FZ, L), F32)
    for f in range(F):
        for h in range(2):
            g = f * 2 + h
            acc = jnp.where(group == g, pltpu.roll(ch[f, h * 40 : h * 40 + 40, :], (4 + 8 * g) % L, 1), acc)
    mca[40:80, :] = acc
    mcb[40:80, :] = acc


def ring_sum_diff(tiles_sum, tiles_diff, lane):
    def shifted(tiles):
        up = [pltpu.roll(t, L - 1, 1) for t in tiles]
        down = [pltpu.roll(t, 1, 1) for t in tiles]
        n = len(tiles)
        up = [jnp.where(lane < L - 1, up[t], up[(t + 1) % n]) for t in range(n)]
        down = [jnp.where(lane > 0, down[t], down[(t - 1) % n]) for t in range(n)]
        return up, down

    a, b = shifted(tiles_sum)
    c, d = shifted(tiles_diff)
    return [p + q for p, q in zip(a, b)], [p - q for p, q in zip(c, d)]


def vector_piece(load, own, nt, inv2j, invjj, h, lane):
    ia = 1.0 / (h * h)
    q = 0.25 * ia
    s = 0.5 / h
    cache = {}

    def u(i, r, t, dz=0):
        key = (i, r, t, dz)
        if key not in cache:
            cache[key] = load(i, r, t, dz)
        return cache[key]

    grads = {}

    def g(i, r, t):
        key = (i, r, t)
        if key not in grads:
            grads[key] = (u(i, r, t, 1) - u(i, r, t, -1)) * (inv2j(r, t) * s)
        return grads[key]

    out = {}
    ts = range(nt)
    for r in own:
        inner = (
            [q * (u(1, r + 1, t) - u(1, r - 1, t)) for t in ts],
            [q * (u(0, r + 1, t) - u(0, r - 1, t)) + g(2, r, t) for t in ts],
            [g(1, r, t) for t in ts],
        )
        for i in range(3):
            side, mixed = ring_sum_diff([u(i, r, t) for t in ts], inner[i], lane)
            for t in ts:
                c = u(i, r, t)
                c2 = c + c
                xx = (u(i, r + 1, t) + u(i, r - 1, t) - c2) * ia
                yy = (side[t] - c2) * ia
                zz = (u(i, r, t, 1) + u(i, r, t, -1) - c2) * invjj(r, t)
                cross = mixed[t]
                if i == 0:
                    cross = cross + (g(2, r + 1, t) - g(2, r - 1, t))
                if i == 2:
                    cross = cross + (g(0, r + 1, t) - g(0, r - 1, t))
                out[i, r, t] = (c2, xx + yy + zz, (xx, yy, zz)[i] + cross)
    return out


def interpolate(cc, spread, edges, lane8):
    left, right, low, high = edges
    a, b, c = cc[0], cc[1], cc[2]
    zero = jnp.zeros_like(a)
    mixes = [
        jnp.where(left, 0.75 * a + 0.25 * b, zero),
        0.75 * b + 0.25 * a,
        0.75 * b + 0.25 * c,
        jnp.where(right, 0.75 * c + 0.25 * b, zero),
    ]
    plane = exact_dot(jnp.concatenate(mixes, axis=0), spread[...])
    keep = (lane8 < 2 * L) | ((lane8 < 2 * L + 64) & high) | ((lane8 >= 2 * L + 64) & low)
    return jnp.where(keep, plane, 0.0)


def edges_here():
    x, y = lax.axis_index("gx"), lax.axis_index("gy")
    return x > 0, x < lax.axis_size("gx") - 1, y > 0, y < lax.axis_size("gy") - 1


def fill_ghosts(U, V, cc, spread, edges):
    cc[...] = jnp.zeros_like(cc)
    for f in range(3):
        for r in range(3):
            for t in range(2):
                cc[r, f : f + 1, t * L : (t + 1) * L] = V[f, r, t, ZP : ZP + 1, :]
    plane = interpolate(cc, spread, edges, lanes((32, 384)))
    for f in range(3):
        for r in range(4):
            for t in range(3):
                U[f, r, t, ZP + FZ : ZP + FZ + 1, :] = plane[r * 8 + f : r * 8 + f + 1, t * L : (t + 1) * L]
                U[f, r, t, ZP - 1 : ZP, :] = U[f, r, t, ZP : ZP + 1, :]
        for r in range(3):
            for t in range(2):
                V[f, r, t, ZP + CZ : ZP + CZ + 1, :] = jnp.zeros((1, L), F32)


def one_field(kernel, a):
    def body(*refs):
        kernel(a, *refs)

    body.__name__ = kernel.__name__
    return body


def fine_pieces(U, jv, lane):
    for k in range(FZ // 8):
        at = ZP + 8 * k
        parts = vector_piece(
            lambda i, r, t, dz: U[i, r, t, at + dz : at + dz + 8, :], (1, 2), 3,
            lambda r, t: jv[0, r, t], lambda r, t: jv[1, r, t], 1.0, lane,
        )
        for (i, r, t), values in parts.items():
            yield k, i, r - 1, t, values


def coarse_pieces(V, lane):
    for k in range(CZ // 8):
        at = ZP + 8 * k
        parts = vector_piece(
            lambda i, r, t, dz: V[i, r, t, at + dz : at + dz + 8, :], (1,), 2,
            lambda r, t: 0.25, lambda r, t: 0.25, 2.0, lane,
        )
        for (i, r, t), values in parts.items():
            yield k, i, t, values


def fill_one(a, fn, cn, tp, fh, th, ch, rg, rxa, rxb, rca, rcb, jv, U, V, heights):
    px = lax.rem(lax.axis_index("gx"), 2)
    near40 = ((lanes((FZ, L)) + 4) & 127) < 8

    def corner(rc, part, g):
        return jnp.where(near40, pltpu.roll(rc[part * 40 : part * 40 + 40, :], (2 * L - 4 - 8 * g) % L, 1), 0.0)

    body = slice(ZP, ZP + FZ)
    for i in range(3):
        f = 3 * a + i
        for x in range(2):
            for t in range(2):
                U[i, 1 + x, t, body, :] = fn[fine_rows(f, t, x), :]
            U[i, 1 + x, 2, body, :] = fh[f * 2 + x]
        V[i, 1, 0, ZP : ZP + CZ, :] = cn[f * CZ : (f + 1) * CZ, :]
        V[i, 1, 1, ZP : ZP + CZ, :] = ch[f]
        for t in range(2):
            V[i, 1, t, ZP - 1 : ZP, :] = rg[f : f + 1, t * L : (t + 1) * L]
    for rx, rc, fr, cr in ((rxa.at[a * HALF : (a + 1) * HALF, :], rca, 3 * (1 - px), 2 * (1 - px)), (rxb, rcb, 3 * px, 2 * px)):
        for i in range(3):
            f = 3 * a + i
            for t in range(2):
                U[i, fr, t, body, :] = rx[i * 80 + t * 40 : i * 80 + t * 40 + 40, :]
            U[i, fr, 2, body, :] = corner(rc, 0, f)
            V[i, cr, 0, ZP : ZP + CZ, :] = rx[HCOARSE + i * CZ : HCOARSE + (i + 1) * CZ, :]
            for half in range(2):
                V[i, cr, 1, ZP + half * 40 : ZP + half * 40 + 40, :] = corner(rc, 1, f * 2 + half)
            V[i, cr, 0, ZP - 1 : ZP, :] = rx[HFINE + i : HFINE + i + 1, :]
            V[i, cr, 1, ZP - 1 : ZP, :] = corner(rc, 0, 7 + f)[0:1, :]
        if heights:
            for t in range(2):
                jv[0, fr, t] = jnp.broadcast_to(rx[HTOPO + t : HTOPO + t + 1, :], (8, L))
            jv[0, fr, 2] = corner(rc, 0, 6)[0:8, :]
    if heights:
        for x in range(2):
            for t in range(2):
                jv[0, 1 + x, t] = jnp.broadcast_to(tp[t * 2 + x : t * 2 + x + 1, :].astype(F32), (8, L))
            jv[0, 1 + x, 2] = th[x]


def spacings(jv):
    for r in range(4):
        for t in range(3):
            spacing = 1.0 + jv[0, r, t] * (1.0 / 1024.0)
            jv[0, r, t] = 1.0 / (2.0 * spacing)
            jv[1, r, t] = 1.0 / (spacing * spacing)


def tables(sf, lf, sc, lc, sh, sch, jv, cf, cv):
    spacings(jv)
    for x in range(2):
        for t in range(3):
            shear = sf[coef_rows(t, x), :] if t < 2 else sh[x]
            lame = lf[coef_rows(t, x), :] if t < 2 else sh[2 + x]
            cf[0, x, t] = DT2 * shear
            cf[1, x, t] = DT2 * (lame + shear)
    for t in range(2):
        shear = sc[...] if t == 0 else sch[0]
        lame = lc[...] if t == 0 else sch[1]
        cv[0, t] = DT2 * shear
        cv[1, t] = DT2 * (lame + shear)


def step_one(
    a, fn, fo, cn, co, sf, lf, sc, lc, tp, fh, foh, sh, th, ch, coh, sch, rg, rxa, rxb, rca, rcb, spread, pool,
    f1, c1, c1h, rg1, mxa, jv, cf, cv, U, V, cc, tmp,
):
    px = lax.rem(lax.axis_index("gx"), 2)
    edges = edges_here()
    lane = lanes((8, L))
    lane40 = lanes((FZ, L))
    fill_one(a, fn, cn, tp, fh, th, ch, rg, rxa, rxb, rca, rcb, jv, U, V, a == 0)
    if a == 0:
        tables(sf, lf, sc, lc, sh, sch, jv, cf, cv)
    fill_ghosts(U, V, cc, spread, edges)
    keep = ((lane < 64) & edges[3]) | ((lane >= 64) & edges[2])
    for k, i, x, t, (c2, lap, gd) in fine_pieces(U, jv, lane):
        f = 3 * a + i
        zs = slice(8 * k, 8 * k + 8)
        old = fo[fine_rows(f, t, x, 8 * k, 8), :] if t < 2 else foh[f * 2 + x, zs, :]
        new = c2 - old + cf[0, x, t, zs, :] * lap + cf[1, x, t, zs, :] * gd
        f1[i * 2 + x, t, zs, :] = new if t < 2 else jnp.where(keep, new, 0.0)
    for k, i, t, (c2, lap, gd) in coarse_pieces(V, lane):
        f = 3 * a + i
        zs = slice(8 * k, 8 * k + 8)
        old = co[f * CZ + 8 * k : f * CZ + 8 * k + 8, :] if t == 0 else coh[f, zs, :]
        new = c2 - old + cv[0, t, zs, :] * lap + cv[1, t, zs, :] * gd
        if t == 0:
            c1[i * CZ + 8 * k : i * CZ + 8 * k + 8, :] = new
        else:
            c1h[i, zs, :] = jnp.where(keep, new, 0.0)
    tmp[...] = jnp.zeros_like(tmp)
    for i in range(3):
        for t in range(3):
            tmp[i : i + 1, t * L : (t + 1) * L] = f1[i * 2, t, FZ - 1 : FZ, :] + f1[i * 2 + 1, t, FZ - 1 : FZ, :]
    rg1[...] = exact_dot(tmp[...], pool[...])
    row = 1 - px
    for i in range(3):
        for t in range(2):
            mxa[i * 80 + t * 40 : i * 80 + t * 40 + 40, :] = f1[i * 2 + row, t]
    mxa[HFINE:HCOARSE, :] = rg1[:, 0:L]
    mxa[HCOARSE:HLATER, :] = later_corners([f1[i * 2 + row, 2] for i in range(3)], c1h, lane40)


def step_one_both(
    fn, fo, cn, co, sf, lf, sc, lc, tp, fh, foh, sh, th, ch, coh, sch, rg, rxa, rxf, rxg, rca, rcb, spread, pool,
    f1f, c1f, c1hf, rgf, f1g, c1g, c1hg, rgg, mxf, mxg, jv, cf, cv, U, V, cc, tmp,
):
    fields = ((f1f, c1f, c1hf, rgf), (f1g, c1g, c1hg, rgg))
    for a, rxb in enumerate((rxf, rxg)):
        step_one(
            a, fn, fo, cn, co, sf, lf, sc, lc, tp, fh, foh, sh, th, ch, coh, sch, rg, rxa, rxb, rca, rcb, spread, pool,
            *fields[a], (mxf, mxg)[a], jv, cf, cv, U, V, cc, tmp,
        )


def rush(
    a, fn, fo, cn, co, sf, lf, sc, lc, tp, fh, foh, sh, th, ch, coh, sch, rg, rxa, rxb, rca, rcb, spread, pool,
    mxb, jv, U, V, cc, tmp, beside_fine, beside_coarse, bottoms,
):
    px = lax.rem(lax.axis_index("gx"), 2)
    edges = edges_here()
    lane = lanes((8, L))
    lane40 = lanes((FZ, L))
    keep = ((lane < 64) & edges[3]) | ((lane >= 64) & edges[2])
    bottoms[...] = jnp.zeros_like(bottoms)
    fill_one(a, fn, cn, tp, fh, th, ch, rg, rxa, rxb, rca, rcb, jv, U, V, True)
    spacings(jv)
    fill_ghosts(U, V, cc, spread, edges)

    def stepped(c2, old, shear, lame, lap, gd):
        return c2 - old + (DT2 * shear) * lap + (DT2 * (lame + shear)) * gd

    for near, x, ks in ((0, px, range(FZ // 8)), (1, 1 - px, (FZ // 8 - 1,))):
        for k in ks:
            at = ZP + 8 * k
            zs = slice(8 * k, 8 * k + 8)
            parts = vector_piece(
                lambda i, r, t, dz: U[i, x + r, t, at + dz : at + dz + 8, :], (1,), 3,
                lambda r, t: jv[0, x + r, t], lambda r, t: jv[1, x + r, t], 1.0, lane,
            )
            for (i, r, t), (c2, lap, gd) in parts.items():
                f = 3 * a + i
                if t < 2:
                    rows = coef_rows(t, x, 8 * k, 8)
                    new = stepped(c2, fo[fine_rows(f, t, x, 8 * k, 8), :], sf[rows, :], lf[rows, :], lap, gd)
                else:
                    new = stepped(c2, foh[f * 2 + x, zs, :], sh[x, zs, :], sh[2 + x, zs, :], lap, gd)
                    new = jnp.where(keep, new, 0.0)
                if near == 0:
                    if t < 2:
                        mxb[i * 80 + t * 40 + 8 * k : i * 80 + t * 40 + 8 * k + 8, :] = new
                    else:
                        beside_fine[i, zs, :] = new
                if k == FZ // 8 - 1:
                    bottoms[near, i : i + 1, t * L : (t + 1) * L] = new[7:8, :]
    for k, i, t, (c2, lap, gd) in coarse_pieces(V, lane):
        zs = slice(8 * k, 8 * k + 8)
        f = 3 * a + i
        if t == 0:
            new = stepped(c2, co[f * CZ + 8 * k : f * CZ + 8 * k + 8, :], sc[zs, :], lc[zs, :], lap, gd)
            mxb[HLATER + i * CZ + 8 * k : HLATER + i * CZ + 8 * k + 8, :] = new
        else:
            new = stepped(c2, coh[f, zs, :], sch[0, zs, :], sch[1, zs, :], lap, gd)
            beside_coarse[i, zs, :] = jnp.where(keep, new, 0.0)
    mxb[HFINE:HCOARSE, :] = exact_dot(bottoms[0] + bottoms[1], pool[:, 0:L])
    mxb[HCOARSE:HLATER, :] = later_corners([beside_fine[i] for i in range(3)], beside_coarse, lane40)


def later_corners(beside, c1h, lane40):
    group = lane40 >> 2
    acc = jnp.zeros((FZ, L), F32)
    for i in range(3):
        acc = jnp.where(group == i, pltpu.roll(beside[i], 2 + 4 * i, 1), acc)
        for half in range(2):
            g = 3 + 2 * i + half
            acc = jnp.where(group == g, pltpu.roll(c1h[i, half * 40 : half * 40 + 40, :], 2 + 4 * g, 1), acc)
    return acc


def step_two(a, fn, cn, f1, c1, c1h, rg1, rxa, rac, rxb, jv, cf, cv, spread, fout, cout, U, V, cc, after_fine=None):
    px = lax.rem(lax.axis_index("gx"), 2)
    edges = edges_here()
    lane = lanes((8, L))
    near40 = ((lanes((FZ, L)) + 2) & 127) < 4

    def corner(rx, g):
        return jnp.where(near40, pltpu.roll(rx[HCOARSE:HLATER, :], (2 * L - 2 - 4 * g) % L, 1), 0.0)

    cc[...] = jnp.zeros_like(cc)
    body = slice(ZP, ZP + FZ)
    for i in range(3):
        for x in range(2):
            for t in range(3):
                U[i, 1 + x, t, body, :] = f1[i * 2 + x, t]
        V[i, 1, 0, ZP : ZP + CZ, :] = c1[i * CZ : (i + 1) * CZ, :]
        V[i, 1, 1, ZP : ZP + CZ, :] = c1h[i]
        for t in range(2):
            V[i, 1, t, ZP - 1 : ZP, :] = rg1[i : i + 1, t * L : (t + 1) * L]
    for rx, rz, zat, fr, cr in ((rxa, rac, 0, 3 * (1 - px), 2 * (1 - px)), (rxb, rxb, HLATER, 3 * px, 2 * px)):
        for i in range(3):
            for t in range(2):
                U[i, fr, t, body, :] = rx[i * 80 + t * 40 : i * 80 + t * 40 + 40, :]
            U[i, fr, 2, body, :] = corner(rx, i)
            V[i, cr, 0, ZP : ZP + CZ, :] = rz[zat + i * CZ : zat + (i + 1) * CZ, :]
            for half in range(2):
                V[i, cr, 1, ZP + half * 40 : ZP + half * 40 + 40, :] = corner(rx, 3 + i * 2 + half)
            V[i, cr, 0, ZP - 1 : ZP, :] = rx[HFINE + i : HFINE + i + 1, :]
            V[i, cr, 1, ZP - 1 : ZP, :] = jnp.zeros((1, L), F32)
    fill_ghosts(U, V, cc, spread, edges)
    for k, i, x, t, (c2, lap, gd) in fine_pieces(U, jv, lane):
        if t < 2:
            zs = slice(8 * k, 8 * k + 8)
            old = fn[fine_rows(3 * a + i, t, x, 8 * k, 8), :]
            fout[fine_rows(i, t, x, 8 * k, 8), :] = c2 - old + cf[0, x, t, zs, :] * lap + cf[1, x, t, zs, :] * gd
    if after_fine is not None:
        after_fine()
    for k, i, t, (c2, lap, gd) in coarse_pieces(V, lane):
        if t == 0:
            zs = slice(8 * k, 8 * k + 8)
            f = 3 * a + i
            old = cn[f * CZ + 8 * k : f * CZ + 8 * k + 8, :]
            cout[i * CZ + 8 * k : i * CZ + 8 * k + 8, :] = c2 - old + cv[0, t, zs, :] * lap + cv[1, t, zs, :] * gd


def step_two_first(fn, cn, f1, c1, c1h, rg1, rxa, rac, rxb, jv, cf, cv, spread, f1g, c1g, fout, cout, fk1, ck1, U, V, cc):
    step_two(0, fn, cn, f1, c1, c1h, rg1, rxa, rac, rxb, jv, cf, cv, spread, fout, cout, U, V, cc)
    for q in range(4):
        x, t = q // 2, q % 2
        total = jnp.zeros((FZ, L), F32)
        for i in range(3):
            total = total + f1[i * 2 + x, t] * f1g[i * 2 + x, t]
        fk1[q] = total
    total = jnp.zeros((CZ, L), F32)
    for i in range(3):
        total = total + c1[i * CZ : (i + 1) * CZ, :] * c1g[i * CZ : (i + 1) * CZ, :]
    ck1[...] = total


def step_two_last(
    fn, cn, f1, c1, c1h, rg1, rxa, rac, rxb, jv, cf, cv, spread, fof, cof, fk1, ck1,
    fout, cout, fk, ck, U, V, cc, fog, cog, fks, cks, sems,
):
    half_f, half_c = 3 * FZ * 4, 3 * CZ
    copies = [
        pltpu.make_async_copy(fof, fout.at[0:half_f, :], sems.at[0]),
        pltpu.make_async_copy(cof, cout.at[0:half_c, :], sems.at[1]),
        pltpu.make_async_copy(fog, fout.at[half_f : 2 * half_f, :], sems.at[2]),
        pltpu.make_async_copy(cog, cout.at[half_c : 2 * half_c, :], sems.at[3]),
        pltpu.make_async_copy(fks, fk, sems.at[4]),
        pltpu.make_async_copy(cks, ck, sems.at[5]),
    ]
    copies[0].start()
    copies[1].start()

    def fine_done():
        copies[2].start()

    step_two(1, fn, cn, f1, c1, c1h, rg1, rxa, rac, rxb, jv, cf, cv, spread, fog, cog, U, V, cc, fine_done)
    copies[3].start()
    total = ck1[...]
    for i in range(3):
        total = total + cof[i * CZ : (i + 1) * CZ, :] * cog[i * CZ : (i + 1) * CZ, :]
    cks[...] = total
    copies[5].start()
    for x in range(2):
        for t in range(2):
            total = fk1[x * 2 + t]
            for i in range(3):
                total = total + fof[fine_rows(i, t, x), :] * fog[fine_rows(i, t, x), :]
            fks[coef_rows(t, x), :] = total
    copies[4].start()
    for copy in copies:
        copy.wait()


def call(kernel, args, outs, scratch, space=VM, megabytes=12, flops=0, out_space=VM):
    shapes = tuple(jax.ShapeDtypeStruct(s, F32) if isinstance(s, tuple) else s for s in outs)
    return pl.pallas_call(
        kernel,
        out_shape=shapes,
        in_specs=[space] * len(args),
        out_specs=(out_space,) * len(outs),
        scratch_shapes=[pltpu.VMEM(s, F32) if isinstance(s, tuple) else s for s in scratch],
        cost_estimate=pl.CostEstimate(flops=flops, transcendentals=0, bytes_accessed=1024) if flops else None,
        compiler_params=pltpu.CompilerParams(vmem_limit_bytes=megabytes * 1024 * 1024),
    )(*args)


def swap(cells, axis, first):
    count = lax.axis_size(axis)
    return lax.ppermute(cells, axis, [p for i in range(first, count - 1, 2) for p in ((i, i + 1), (i + 1, i))])


def rows_of(array):
    lead = array.size // 512
    return array.reshape(lead, 2, 2, L).transpose(0, 2, 1, 3).reshape(lead * 4, L)


def fine_of(rows, shape):
    return rows.reshape(-1, 2, 2, L).transpose(0, 2, 1, 3).reshape(shape)


def on_device(fine_old, fine_now, coarse_old, coarse_now, shear_fine, lame_fine, shear_coarse, lame_coarse, topography):
    fo, fn, sf, lf = rows_of(fine_old), rows_of(fine_now), rows_of(shear_fine), rows_of(lame_fine)
    tp = rows_of(topography)
    co, cn = coarse_old.reshape(-1, L), coarse_now.reshape(-1, L)
    sc, lc = shear_coarse.reshape(-1, L), lame_coarse.reshape(-1, L)
    pool, spread = jnp.asarray(POOL), jnp.asarray(SPREAD)
    raw = (fn, fo, cn, co, sf, lf, sc, lc, tp, pool, spread)
    raw = tuple(pltpu.with_memory_space_constraint(v, pltpu.HBM) for v in raw)
    local = call(
        load_and_pack_y,
        raw,
        tuple(jax.ShapeDtypeStruct(v.shape, v.dtype) for v in raw) + ((2 * HALF, L), (HALF + 8, L), (HALF + 8, L), (80, L), (80, L)),
        ((8, 256), pltpu.SemaphoreType.DMA((len(raw),)),),
        pl.BlockSpec(memory_space=pltpu.HBM),
    )
    fn, fo, cn, co, sf, lf, sc, lc, tp, pool, spread, ma, mbf, mbg, mya, myb = local
    ryb = swap(myb, "gy", 1)
    rya = swap(mya, "gy", 0)
    by_link = [swap(m, "gx", 1) for m in (mbf, mbg)]
    in_chip = swap(ma, "gx", 0)
    fh, foh, sh, th, ch, coh, sch, rg, mca, mcb = call(
        open_y,
        (ryb, rya, fn, pool),
        ((12, FZ, L), (12, FZ, L), (4, FZ, L), (2, 8, L), (F, CZ, L), (F, CZ, L), (2, CZ, L), (8, 256), (80, L), (80, L)),
        ((8, 384),),
        flops=C_OPEN,
    )
    rcb = swap(mcb, "gx", 1)
    rca = swap(mca, "gx", 0)
    field = ((3, 4, 3, 56, L), (3, 3, 2, 96, L), (3, 8, 256))
    far = []
    for a in range(2):
        (mxb,) = call(
            one_field(rush, a),
            (fn, fo, cn, co, sf, lf, sc, lc, tp, fh, foh, sh, th, ch, coh, sch, rg, in_chip, by_link[a], rca, rcb, spread, pool),
            ((HALF + 40, L),),
            ((2, 4, 3, 8, L), *field, (8, 384), (3, FZ, L), (3, CZ, L), (2, 8, 384)),
            flops=C_ONE[a],
        )
        far.append(swap(mxb, "gx", 1))
    first = ((6, 3, FZ, L), (3 * CZ, L), (3, CZ, L), (8, 256))
    *results, mxf, mxg, jv, cf, cv = call(
        step_one_both,
        (fn, fo, cn, co, sf, lf, sc, lc, tp, fh, foh, sh, th, ch, coh, sch, rg, in_chip, *by_link, rca, rcb, spread, pool),
        first + first + ((HLATER, L), (HLATER, L), (2, 4, 3, 8, L), (2, 2, 3, FZ, L), (2, 2, CZ, L)),
        field + ((8, 384),),
        flops=C_BOTH,
    )
    firsts = (results[:4], results[4:])
    near = [(swap(m, "gx", 0), swap(r[1], "gx", 0)) for m, r in zip((mxf, mxg), firsts)]
    fof, cof, fk1, ck1 = call(
        step_two_first,
        (fn, cn, *firsts[0], *near[0], far[0], jv, cf, cv, spread, *firsts[1][:2]),
        ((3 * FZ * 4, L), (3 * CZ, L), (4, FZ, L), (CZ, L)),
        field,
        flops=C_TWO,
    )
    fout, cout, fk, ck = call(
        step_two_last,
        (fn, cn, *firsts[1], *near[1], far[1], jv, cf, cv, spread, fof, cof, fk1, ck1),
        ((FINE_ROWS, L), (COARSE_ROWS, L), (4 * FZ, L), (CZ, L)),
        field + ((3 * FZ * 4, L), (3 * CZ, L), (4 * FZ, L), (CZ, L), pltpu.SemaphoreType.DMA((6,))),
        out_space=pl.BlockSpec(memory_space=pltpu.HBM),
    )
    return (
        fine_of(fout, fine_now.shape),
        cout.reshape(coarse_now.shape),
        fine_of(fk, shear_fine.shape),
        ck.reshape(shear_coarse.shape),
    )


def solution(mesh):
    fields = P(None, None, None, "gx", "gy")
    cells = P(None, "gx", "gy")
    return jax.shard_map(
        on_device,
        mesh=mesh,
        in_specs=(fields, fields, fields, fields, cells, cells, cells, cells, P("gx", "gy")),
        out_specs=(fields, fields, cells, cells),
        check_vma=False,
    )
```
